32 devices in a mesh: group: 4 (over y, x), member: 8 (over z, core).
Axes of the slice: x: 2, y: 2, z: 4, core: 2. Of those that a mesh axis runs over, the one named last changes fastest.
Arguments:
- features: bfloat16 [131072, 128], P(('group', 'member')), may hold values from -6 to 6
- history: bfloat16 [131072, 128], P(('group', 'member')), may hold values from -6 to 6
- tiles: bfloat16 [16384, 128, 128], P(('group', 'member'))
- tile_src: int32 [1024, 16], P(('group', 'member')), may hold values from 0 to 47
- degree: int32 [131072], P(('group', 'member')), may hold values from 8 to 128
- boundary_rows: int32 [32, 256], P(('group', 'member')), may hold values from 0 to 4095
- picks: int32 [256, 1], P(('group', 'member')), may hold values from 0 to 1
- stale_rows: int32 [128, 256], P(('group', 'member')), may hold values from 0 to 4095
- w_self: bfloat16 [128, 128], replicated, may hold values from -0.5 to 0.5
- w_neigh: bfloat16 [128, 128], replicated, may hold values from -0.5 to 0.5
- cotangent: bfloat16 [131072, 128], P(('group', 'member')), may hold values from -6 to 6
Outputs:
- layer_out: bfloat16 [131072, 128], P(('group', 'member'))
- grad_features: bfloat16 [131072, 128], P(('group', 'member'))
- grad_self: float32 [128, 128], replicated
- grad_neigh: float32 [128, 128], replicated
The draws below stay inside these ranges and needn't reach their ends.
Inputs may be any that keep to these rules, and one draw needn't show every extreme that they name: `boundary_rows`: local row indices of the sending device. `stale_rows`: local row indices of the sending device, one list for each destination group. `tile_src`: indices into the device's source blocks: own blocks, then taken boundary blocks member by member, then historical blocks group by group. `degree`: a normalizer given with the graph, not derived from the tiles.
All inputs are finite; a program needn't handle non-finite values.
Results may differ from the reference program's by a relative error of at most 0.0051.
Values may be sent and summed in bfloat16 or wider, within the bound.
A program may use at most 192 MiB of HBM per device.

```python
import jax
import jax.numpy as jnp
from jax import lax

WIDTH = 128
OUT_WIDTH = 128
TILE = 128
BLOCKS_DEV = 32
TILES_ROW = 16
PICKED = 1
BOUNDARY = 2
STALE = 2
NODES_DEV = 4096
NODES = 131072
BLOCKS = 1024
SOURCES = 48
N_GROUP = 4
N_MEMBER = 8
DEVICES = 32


def draw_tiles(key, part):
    first, second = jax.random.split(jax.random.fold_in(key, 17))
    shape = (BLOCKS * TILES_ROW, TILE, TILE)
    density = 0.0625
    values = jax.random.uniform(second, shape, jnp.float32, 0.5, 1.5)
    keep = jax.random.uniform(first, shape, jnp.float32) < density
    return jnp.where(keep, values, 0.0).astype(jnp.bfloat16)


def plant(drawn, rng, low, largest):
    index_at = [jax.random.randint(jax.random.fold_in(rng, axis), (), 0, length) for axis, length in enumerate(drawn.shape)]
    main_axis = drawn.shape.index(max(drawn.shape))
    next_to = index_at[:main_axis] + [(index_at[main_axis] + 1) % drawn.shape[main_axis]] + index_at[main_axis + 1:]
    return drawn.at[tuple(index_at)].set(low).at[tuple(next_to)].set(largest)


def block_scale(stream_key, dims, shards, low, top_value):
    gain, own = 1.0, jax.random.fold_in(stream_key, 6)
    for position, shards_of in shards:
        heights = jnp.exp(jax.random.uniform(jax.random.fold_in(own, position), (shards_of,), jnp.float32, low / len(shards), top_value / len(shards)))
        gain = gain * jnp.repeat(heights, dims[position] // shards_of).reshape([-1 if axis == position else 1 for axis in range(len(dims))])
    return gain


def noise(rng, dims, width, most, cuts=(), kind=jnp.bfloat16):
    values = jax.random.normal(rng, dims, jnp.float32) * width
    if len(cuts) > 0:
        values = block_scale(rng, dims, cuts, -0.22, 0.18) * values
    return jnp.clip(values, min=-most, max=most).astype(kind)


def setup_inputs(seed: int = 0) -> dict:
    splits = jax.random.split(jax.random.key(seed), 12)
    features = noise(splits[0], (NODES, WIDTH), 1.0, 6.0, ((0, 32),))
    history = noise(splits[1], (NODES, WIDTH), 1.0, 6.0, ((0, 32),))
    tiles = draw_tiles(jax.random.fold_in(splits[11], 71), 0)
    tile_src = plant(jax.random.randint(splits[3], (BLOCKS, TILES_ROW), 0, SOURCES), jax.random.fold_in(splits[3], 1), 0, SOURCES - 1).astype(jnp.int32)
    degree = plant(jax.random.randint(splits[4], (NODES,), 8, 129), jax.random.fold_in(splits[4], 1), 8, 128).astype(jnp.int32)
    boundary_rows = plant(jax.random.randint(splits[5], (DEVICES, BOUNDARY * TILE), 0, NODES_DEV), jax.random.fold_in(splits[5], 1), 0, NODES_DEV - 1).astype(jnp.int32)
    picks = plant(jax.random.randint(splits[6], (DEVICES * N_MEMBER, PICKED), 0, BOUNDARY), jax.random.fold_in(splits[6], 1), 0, BOUNDARY - 1).astype(jnp.int32)
    stale_rows = plant(jax.random.randint(splits[7], (DEVICES * N_GROUP, STALE * TILE), 0, NODES_DEV), jax.random.fold_in(splits[7], 1), 0, NODES_DEV - 1).astype(jnp.int32)
    w_self = noise(splits[8], (WIDTH, OUT_WIDTH), WIDTH ** -0.5, 0.5)
    w_neigh = noise(splits[9], (WIDTH, OUT_WIDTH), WIDTH ** -0.5, 0.5)
    cotangent = noise(splits[10], (NODES, OUT_WIDTH), 1.0, 6.0, ((0, 32),))
    return dict(features=features, history=history, tiles=tiles, tile_src=tile_src, degree=degree, boundary_rows=boundary_rows, picks=picks, stale_rows=stale_rows, w_self=w_self, w_neigh=w_neigh, cotangent=cotangent)


def reference(features, history, tiles, tile_src, degree, boundary_rows, picks, stale_rows, w_self, w_neigh, cotangent):
    groups = N_GROUP
    members = N_MEMBER
    devs = groups * members
    feats = features.reshape(devs, NODES_DEV, WIDTH)
    hists = history.reshape(devs, NODES_DEV, WIDTH)
    brows = boundary_rows.reshape(devs, BOUNDARY * TILE)
    bound = jax.vmap(lambda table, rows: table[rows])(feats, brows).reshape(devs, BOUNDARY, TILE, WIDTH)
    chosen = picks.reshape(devs, members, PICKED)
    group_of = jnp.arange(devs, dtype=jnp.int32) // members
    owner = group_of[:, None] * members + jnp.arange(members, dtype=jnp.int32)[None, :]
    halo = bound[owner[:, :, None], chosen]
    srows = stale_rows.reshape(devs, groups, STALE * TILE)
    sent = jax.vmap(lambda table, rows: table[rows])(hists, srows)
    sent = sent.reshape(groups, members, groups, STALE, TILE, WIDTH)
    stale = sent.transpose(2, 1, 0, 3, 4, 5).reshape(devs, groups * STALE, TILE, WIDTH)
    sources = jnp.concatenate([feats.reshape(devs, BLOCKS_DEV, TILE, WIDTH), halo.reshape(devs, members * PICKED, TILE, WIDTH), stale], axis=1)
    tiled = tiles.reshape(devs, BLOCKS_DEV, TILES_ROW, TILE, TILE)
    src_index = tile_src.reshape(devs, BLOCKS_DEV, TILES_ROW)
    degs = degree.reshape(devs, NODES_DEV, 1).astype(jnp.float32)
    cots = cotangent.reshape(devs, NODES_DEV, OUT_WIDTH)

    def one_device(args):
        srcs, tl, idx, dg, own, cot = args
        picked = srcs[idx]
        summed = jnp.einsum('btij,btjf->bif', tl.astype(jnp.float32), picked.astype(jnp.float32))
        agg = (summed.reshape(NODES_DEV, WIDTH) / dg).astype(jnp.bfloat16)
        pre = jnp.dot(own, w_self, preferred_element_type=jnp.float32) + jnp.dot(agg, w_neigh, preferred_element_type=jnp.float32)
        scale_row = lax.rsqrt(lax.optimization_barrier(jnp.mean(pre * pre, axis=-1, keepdims=True)) + 1e-05)
        out = (pre * scale_row).astype(jnp.bfloat16)
        grad_out = cot.astype(jnp.float32)
        dpre = (scale_row * grad_out - pre * scale_row ** 3 * lax.optimization_barrier(jnp.mean(grad_out * pre, axis=-1, keepdims=True))).astype(jnp.bfloat16)
        part_self = jnp.dot(own.T, dpre, preferred_element_type=jnp.float32)
        part_neigh = jnp.dot(agg.T, dpre, preferred_element_type=jnp.float32)
        dself = jnp.dot(dpre, w_self.T, preferred_element_type=jnp.float32)
        back = (jnp.dot(dpre, w_neigh.T, preferred_element_type=jnp.float32) / dg).astype(jnp.bfloat16)
        back = back.reshape(BLOCKS_DEV, TILE, WIDTH)
        per_tile = jnp.einsum('btij,bif->btjf', tl.astype(jnp.float32), back.astype(jnp.float32))
        src_grad = jnp.zeros((SOURCES, TILE, WIDTH), jnp.float32).at[idx.reshape(-1)].add(per_tile.reshape(-1, TILE, WIDTH))
        return (out, part_self, part_neigh, dself, src_grad[:BLOCKS_DEV + members * PICKED])
    outs, parts_self, parts_neigh, dselfs, src_grads = lax.map(one_device, (sources, tiled, src_index, degs, feats, cots))
    factor = NODES ** (-0.5)
    grad_self = lax.optimization_barrier(jnp.sum(parts_self, axis=0)) * factor
    grad_neigh = lax.optimization_barrier(jnp.sum(parts_neigh, axis=0)) * factor
    local_grad = src_grads[:, :BLOCKS_DEV].reshape(devs, NODES_DEV, WIDTH)
    halo_grad = src_grads[:, BLOCKS_DEV:].reshape(devs, members, PICKED, TILE, WIDTH)
    bound_grad = jnp.zeros((devs, BOUNDARY, TILE, WIDTH), jnp.float32).at[owner[:, :, None], chosen].add(halo_grad)
    row_grad = dselfs + local_grad
    row_grad = jax.vmap(lambda grads, rows, extra: grads.at[rows].add(extra.reshape(-1, WIDTH)))(row_grad, brows, bound_grad)
    layer_out = outs.reshape(NODES, OUT_WIDTH)
    grad_features = row_grad.reshape(NODES, WIDTH).astype(jnp.bfloat16)
    return (layer_out, grad_features, grad_self, grad_neigh)
```

```python
import functools
import math

import jax
import jax.numpy as jnp
from jax import lax
from jax.experimental import pallas as pl
from jax.experimental.pallas import tpu as pltpu
from jax.sharding import PartitionSpec as P

QUAD = 4
F32 = jnp.float32
BF16 = jnp.bfloat16


def plan(tile_src, wanted_sources):
    flat = tile_src.reshape(-1)
    total = flat.shape[0]
    slots = (total + wanted_sources * (QUAD - 1)) // QUAD * QUAD
    index = jnp.arange(total, dtype=jnp.int32)
    same = flat[:, None] == flat[None, :]
    within = jnp.sum(jnp.where(same & (index[None, :] < index[:, None]), 1, 0), axis=1)
    ids = jnp.arange(wanted_sources, dtype=jnp.int32)
    hit = flat[None, :] == ids[:, None]
    count = jnp.sum(hit.astype(jnp.int32), axis=1)
    padded = (count + QUAD - 1) // QUAD * QUAD
    offset = jnp.sum(jnp.where(ids[None, :] < ids[:, None], padded[None, :], 0), axis=1)
    base = jnp.sum(jnp.where(hit, offset[:, None], 0), axis=0)
    pos = jnp.where(flat < wanted_sources, base + within, -1)
    slot = jnp.arange(slots, dtype=jnp.int32)
    code = jnp.sum(jnp.where(pos[None, :] == slot[:, None], index[None, :] + 1, 0), axis=1)
    first = slot[::QUAD]
    inside = (offset[None, :] <= first[:, None]) & (first[:, None] < (offset + padded)[None, :])
    start = inside & (offset[None, :] == first[:, None])
    quad = jnp.sum(jnp.where(inside, 2 * ids[None, :], 0) + start.astype(jnp.int32), axis=1)
    used = (jnp.sum(padded) // QUAD).reshape(1)
    return code, quad, used


def local_kernel(
    src,
    code,
    quad,
    used,
    feats,
    halo,
    stale,
    tiles,
    deg,
    w_self,
    w_neigh,
    cot,
    out,
    row_grad,
    halo_grad,
    g_self,
    g_neigh,
    tbuf,
    srcs,
    agg,
    back,
    grad,
    gt,
    sems,
):
    blocks, per = src.shape
    tile, width = feats.shape[0] // blocks, feats.shape[1]
    n_halo, n_stale = halo.shape[0], stale.shape[0]

    def chunk(b):
        return pltpu.make_async_copy(
            tiles.at[pl.ds(b * per, per)], tbuf.at[pl.ds(b * per, per)], sems.at[b]
        )

    @pl.loop(0, blocks)
    def _(b):
        chunk(b).start()

    for b in range(blocks):
        srcs[b] = feats[b * tile : (b + 1) * tile, :]
    srcs[blocks : blocks + n_halo] = halo[...]
    srcs[blocks + n_halo :] = stale[...]
    grad[...] = jnp.zeros_like(grad)
    back[blocks] = jnp.zeros((width, tile), BF16)

    def forward(b):
        chunk(b).wait()
        lhs = jnp.concatenate([tbuf[b * per + t] for t in range(per)], axis=1)
        rhs = jnp.concatenate([srcs[src[b, t]] for t in range(per)], axis=0)
        total = jnp.dot(lhs, rhs, preferred_element_type=F32)
        d = jnp.broadcast_to(deg[pl.ds(b, 1), :].astype(F32), (tile, tile)).T
        agg[pl.ds(pl.multiple_of(b * tile, tile), tile), :] = (total / d).astype(BF16)

    pl.loop(0, blocks, unroll=2)(forward)

    gt[...] = jnp.zeros_like(gt)
    group = 4
    rows = group * tile
    w_cat = jnp.concatenate([w_self[...], w_neigh[...]], axis=0)

    def middle(c):
        at = pl.ds(pl.multiple_of(c * rows, rows), rows)
        fa = jnp.concatenate([feats[at, :], agg[at, :]], axis=1)
        pre = jnp.dot(fa, w_cat, preferred_element_type=F32)
        scale = lax.rsqrt(jnp.mean(pre * pre, axis=-1, keepdims=True) + 1e-05)
        out[at, :] = (pre * scale).astype(BF16)
        g = cot[at, :].astype(F32)
        m = jnp.mean(g * pre, axis=-1, keepdims=True)
        dpre = (scale * g - pre * (scale**3 * m)).astype(BF16)
        gt[...] += lax.dot_general(dpre, fa, (((0,), (0,)), ((), ())), preferred_element_type=F32)
        row_grad[at, :] = lax.dot_general(
            dpre, w_self[...], (((1,), (1,)), ((), ())), preferred_element_type=F32
        )
        bt = lax.dot_general(
            w_neigh[...], dpre, (((1,), (1,)), ((), ())), preferred_element_type=F32
        )
        for i in range(group):
            d = deg[pl.ds(c * group + i, 1), :].astype(F32)
            back[c * group + i] = (bt[:, i * tile : (i + 1) * tile] / d).astype(BF16)

    pl.loop(0, blocks // group)(middle)

    g_self[...] = gt[:, :width].T
    g_neigh[...] = gt[:, width:].T

    def backward(q, acc):
        lhs, rhs = [], []
        for i in range(QUAD):
            k = code[q * QUAD + i]
            t = jnp.maximum(k - 1, 0)
            b = jnp.where(k == 0, blocks, t // per)
            lhs.append(back[b])
            rhs.append(tbuf[t])
        term = jnp.dot(
            jnp.concatenate(lhs, axis=1),
            jnp.concatenate(rhs, axis=0),
            preferred_element_type=F32,
        )
        info = quad[q]
        acc = term + jnp.where(info % 2 == 1, 0.0, acc)
        grad[info // 2] = acc
        return acc

    lax.fori_loop(0, used[0], backward, jnp.zeros((width, tile), F32))

    def finish(b):
        at = pl.ds(pl.multiple_of(b * tile, tile), tile)
        row_grad[at, :] += grad[b].T

    pl.loop(0, blocks, unroll=4)(finish)
    for h in range(n_halo):
        halo_grad[h] = grad[blocks + h].T.astype(BF16)


def local(tile_src, plans, features, halo, stale, tiles, degree, w_self, w_neigh, cotangent):
    blocks, per = tile_src.shape
    tile = tiles.shape[1]
    nodes, width = features.shape
    n_halo = halo.shape[0]
    smem = pl.BlockSpec(memory_space=pltpu.SMEM)
    vmem = pl.BlockSpec(memory_space=pltpu.VMEM)
    return pl.pallas_call(
        local_kernel,
        out_shape=(
            jax.ShapeDtypeStruct((nodes, width), BF16),
            jax.ShapeDtypeStruct((nodes, width), F32),
            jax.ShapeDtypeStruct((n_halo, tile, width), BF16),
            jax.ShapeDtypeStruct((width, width), F32),
            jax.ShapeDtypeStruct((width, width), F32),
        ),
        in_specs=[smem] * 4
        + [vmem] * 3
        + [pl.BlockSpec(memory_space=pl.ANY)]
        + [vmem] * 4,
        out_specs=[vmem] * 5,
        scratch_shapes=[
            pltpu.VMEM(tiles.shape, BF16),
            pltpu.VMEM((blocks + n_halo + stale.shape[0], tile, width), BF16),
            pltpu.VMEM((nodes, width), BF16),
            pltpu.VMEM((blocks + 1, width, tile), BF16),
            pltpu.VMEM((blocks + n_halo, width, tile), F32),
            pltpu.VMEM((width, 2 * width), F32),
            pltpu.SemaphoreType.DMA((blocks,)),
        ],
        compiler_params=pltpu.CompilerParams(vmem_limit_bytes=60 << 20),
    )(
        tile_src,
        *plans,
        features,
        halo,
        stale,
        tiles,
        degree.reshape(blocks, tile),
        w_self,
        w_neigh,
        cotangent,
    )


def on_device(
    features,
    history,
    tiles,
    tile_src,
    degree,
    boundary_rows,
    picks,
    stale_rows,
    w_self,
    w_neigh,
    cotangent,
):
    members = lax.axis_size("member")
    groups = lax.axis_size("group")
    tile = tiles.shape[1]
    width = features.shape[1]
    blocks = features.shape[0] // tile
    offered = boundary_rows.shape[1] // tile
    taken = picks.shape[1]
    bound = features[boundary_rows[0]].reshape(offered, tile, width)
    wanted = lax.all_to_all(picks, "member", split_axis=0, concat_axis=0, tiled=True)
    outgoing = bound[wanted]
    halo = lax.all_to_all(outgoing, "member", split_axis=0, concat_axis=0, tiled=True)
    stale = lax.all_to_all(
        history[stale_rows], "group", split_axis=0, concat_axis=0, tiled=True
    ).reshape(-1, tile, width)
    plans = plan(tile_src, blocks + members * taken)
    layer_out, row_grad, halo_grad, part_self, part_neigh = local(
        tile_src,
        plans,
        features,
        halo.reshape(-1, tile, width),
        stale,
        tiles,
        degree,
        w_self,
        w_neigh,
        cotangent,
    )
    returned = lax.all_to_all(
        halo_grad.reshape(members, taken, tile, width),
        "member",
        split_axis=0,
        concat_axis=0,
        tiled=True,
    ).astype(F32)
    bound_grad = jnp.zeros((offered, tile, width), F32).at[wanted].add(returned)
    row_grad = row_grad.at[boundary_rows[0]].add(bound_grad.reshape(-1, width))
    grad_features = row_grad.astype(BF16)
    parts = jnp.concatenate([part_self, part_neigh], axis=0)
    share = lax.psum_scatter(parts, "member", scatter_dimension=0, tiled=True)
    share = lax.psum(share, "group")
    whole = lax.all_gather(share, "member", axis=0, tiled=True)
    factor = 1.0 / math.sqrt(features.shape[0] * members * groups)
    return (layer_out, grad_features, whole[:width] * factor, whole[width:] * factor)


def solution(mesh):
    placed = (
        P(("group", "member"), None),
        P(("group", "member"), None),
        P(("group", "member"), None, None),
        P(("group", "member"), None),
        P(("group", "member")),
        P(("group", "member"), None),
        P(("group", "member"), None),
        P(("group", "member"), None),
        P(),
        P(),
        P(("group", "member"), None),
    )
    return jax.shard_map(
        on_device,
        mesh=mesh,
        in_specs=placed,
        out_specs=(P(("group", "member"), None), P(("group", "member"), None), P(), P()),
        check_vma=False,
    )
```

```python
import functools
import math

import jax
import jax.numpy as jnp
from jax import lax
from jax.experimental import pallas as pl
from jax.experimental.pallas import tpu as pltpu
from jax.sharding import PartitionSpec as P

QUAD = 4
F32 = jnp.float32
BF16 = jnp.bfloat16
MESH = pl.DeviceIdType.MESH


def plan(tile_src, wanted_sources):
    flat = tile_src.reshape(-1)
    total = flat.shape[0]
    slots = (total + wanted_sources * (QUAD - 1)) // QUAD * QUAD
    index = jnp.arange(total, dtype=jnp.int32)
    same = flat[:, None] == flat[None, :]
    within = jnp.sum(jnp.where(same & (index[None, :] < index[:, None]), 1, 0), axis=1)
    ids = jnp.arange(wanted_sources, dtype=jnp.int32)
    hit = flat[None, :] == ids[:, None]
    count = jnp.sum(hit.astype(jnp.int32), axis=1)
    padded = (count + QUAD - 1) // QUAD * QUAD
    offset = jnp.sum(jnp.where(ids[None, :] < ids[:, None], padded[None, :], 0), axis=1)
    base = jnp.sum(jnp.where(hit, offset[:, None], 0), axis=0)
    pos = jnp.where(flat < wanted_sources, base + within, -1)
    slot = jnp.arange(slots, dtype=jnp.int32)
    code = jnp.sum(jnp.where(pos[None, :] == slot[:, None], index[None, :] + 1, 0), axis=1)
    first = slot[::QUAD]
    inside = (offset[None, :] <= first[:, None]) & (first[:, None] < (offset + padded)[None, :])
    start = inside & (offset[None, :] == first[:, None])
    quad = jnp.sum(jnp.where(inside, 2 * ids[None, :], 0) + start.astype(jnp.int32), axis=1)
    used = (jnp.sum(padded) // QUAD).reshape(1)
    return code, quad, used


def local_kernel(
    src,
    code,
    quad,
    used,
    feats,
    halo,
    stale,
    tiles,
    deg,
    w_self,
    w_neigh,
    cot,
    out,
    row_grad,
    halo_grad,
    part,
    tbuf,
    srcs,
    agg,
    back,
    grad,
    gt,
    sems,
):
    blocks, per = src.shape
    tile, width = feats.shape[0] // blocks, feats.shape[1]
    n_halo, n_stale = halo.shape[0], stale.shape[0]

    def chunk(b):
        return pltpu.make_async_copy(
            tiles.at[pl.ds(b * per, per)], tbuf.at[pl.ds(b * per, per)], sems.at[b]
        )

    @pl.loop(0, blocks)
    def _(b):
        chunk(b).start()

    for b in range(blocks):
        srcs[b] = feats[b * tile : (b + 1) * tile, :]
    srcs[blocks : blocks + n_halo] = halo[...]
    srcs[blocks + n_halo :] = stale[...]
    grad[...] = jnp.zeros_like(grad)
    back[blocks] = jnp.zeros((width, tile), BF16)

    def forward(b):
        chunk(b).wait()
        lhs = jnp.concatenate([tbuf[b * per + t] for t in range(per)], axis=1)
        rhs = jnp.concatenate([srcs[src[b, t]] for t in range(per)], axis=0)
        total = jnp.dot(lhs, rhs, preferred_element_type=F32)
        d = jnp.broadcast_to(deg[pl.ds(b, 1), :].astype(F32), (tile, tile)).T
        agg[pl.ds(pl.multiple_of(b * tile, tile), tile), :] = (total / d).astype(BF16)

    pl.loop(0, blocks, unroll=2)(forward)

    gt[...] = jnp.zeros_like(gt)
    group = 4
    rows = group * tile
    w_cat = jnp.concatenate([w_self[...], w_neigh[...]], axis=0)

    def middle(c):
        at = pl.ds(pl.multiple_of(c * rows, rows), rows)
        fa = jnp.concatenate([feats[at, :], agg[at, :]], axis=1)
        pre = jnp.dot(fa, w_cat, preferred_element_type=F32)
        scale = lax.rsqrt(jnp.mean(pre * pre, axis=-1, keepdims=True) + 1e-05)
        out[at, :] = (pre * scale).astype(BF16)
        g = cot[at, :].astype(F32)
        m = jnp.mean(g * pre, axis=-1, keepdims=True)
        dpre = (scale * g - pre * (scale**3 * m)).astype(BF16)
        gt[...] += lax.dot_general(dpre, fa, (((0,), (0,)), ((), ())), preferred_element_type=F32)
        row_grad[at, :] = lax.dot_general(
            dpre, w_self[...], (((1,), (1,)), ((), ())), preferred_element_type=F32
        )
        bt = lax.dot_general(
            w_neigh[...], dpre, (((1,), (1,)), ((), ())), preferred_element_type=F32
        )
        for i in range(group):
            d = deg[pl.ds(c * group + i, 1), :].astype(F32)
            back[c * group + i] = (bt[:, i * tile : (i + 1) * tile] / d).astype(BF16)

    pl.loop(0, blocks // group)(middle)

    part[:width, :] = gt[:, :width].T
    part[width:, :] = gt[:, width:].T

    def backward(q, acc):
        lhs, rhs = [], []
        for i in range(QUAD):
            k = code[q * QUAD + i]
            t = jnp.maximum(k - 1, 0)
            b = jnp.where(k == 0, blocks, t // per)
            lhs.append(back[b])
            rhs.append(tbuf[t])
        term = jnp.dot(
            jnp.concatenate(lhs, axis=1),
            jnp.concatenate(rhs, axis=0),
            preferred_element_type=F32,
        )
        info = quad[q]
        acc = term + jnp.where(info % 2 == 1, 0.0, acc)
        grad[info // 2] = acc
        return acc

    lax.fori_loop(0, used[0], backward, jnp.zeros((width, tile), F32))

    def finish(b):
        at = pl.ds(pl.multiple_of(b * tile, tile), tile)
        row_grad[at, :] += grad[b].T

    pl.loop(0, blocks, unroll=4)(finish)
    for h in range(n_halo):
        halo_grad[h] = grad[blocks + h].T.astype(BF16)


def local(tile_src, plans, features, halo, stale, tiles, degree, w_self, w_neigh, cotangent):
    blocks, per = tile_src.shape
    tile = tiles.shape[1]
    nodes, width = features.shape
    n_halo = halo.shape[0]
    smem = pl.BlockSpec(memory_space=pltpu.SMEM)
    vmem = pl.BlockSpec(memory_space=pltpu.VMEM)
    return pl.pallas_call(
        local_kernel,
        out_shape=(
            jax.ShapeDtypeStruct((nodes, width), BF16),
            jax.ShapeDtypeStruct((nodes, width), F32),
            jax.ShapeDtypeStruct((n_halo, tile, width), BF16),
            jax.ShapeDtypeStruct((2 * width, width), F32),
        ),
        in_specs=[smem] * 4
        + [vmem] * 3
        + [pl.BlockSpec(memory_space=pl.ANY)]
        + [vmem] * 4,
        out_specs=[vmem] * 4,
        scratch_shapes=[
            pltpu.VMEM(tiles.shape, BF16),
            pltpu.VMEM((blocks + n_halo + stale.shape[0], tile, width), BF16),
            pltpu.VMEM((nodes, width), BF16),
            pltpu.VMEM((blocks + 1, width, tile), BF16),
            pltpu.VMEM((blocks + n_halo, width, tile), F32),
            pltpu.VMEM((width, 2 * width), F32),
            pltpu.SemaphoreType.DMA((blocks,)),
        ],
        compiler_params=pltpu.CompilerParams(vmem_limit_bytes=60 << 20),
    )(
        tile_src,
        *plans,
        features,
        halo,
        stale,
        tiles,
        degree.reshape(blocks, tile),
        w_self,
        w_neigh,
        cotangent,
    )


def greet(me_g, me_m, groups, members):
    barrier = pltpu.get_barrier_semaphore()
    for o in range(1, members):
        pl.semaphore_signal(
            barrier, inc=1, device_id=(me_g, lax.rem(me_m + o, members)), device_id_type=MESH
        )
    for o in range(1, groups):
        pl.semaphore_signal(
            barrier, inc=1, device_id=(lax.rem(me_g + o, groups), me_m), device_id_type=MESH
        )
    return lambda: pl.semaphore_wait(barrier, members + groups - 2)


def push(src, dst, send, recv, o, device):
    copy = pltpu.make_async_remote_copy(
        src_ref=src,
        dst_ref=dst,
        send_sem=send.at[o],
        recv_sem=recv.at[o],
        device_id=device,
        device_id_type=MESH,
    )
    copy.start()
    return copy


def pick_rows(row, table, depth):
    count = row.shape[1]
    column = jnp.broadcast_to(row, (8, count)).T[:, :1]
    total = jnp.zeros((count, table.shape[1]), F32)
    for c in range(0, table.shape[0], depth):
        ids = lax.broadcasted_iota(jnp.int32, (count, depth), 1) + c
        hot = jnp.where(ids == column, 1.0, 0.0).astype(BF16)
        total = total + jnp.dot(hot, table[c : c + depth, :], preferred_element_type=F32)
    return total


def gather_kernel(
    groups,
    members,
    feats,
    hist,
    rows,
    picks,
    stale_rows,
    halo,
    stale,
    wanted,
    asked,
    bound,
    outgoing,
    leaving,
    p_send,
    p_recv,
    h_send,
    h_recv,
    s_send,
    s_recv,
):
    me_g, me_m = lax.axis_index("group"), lax.axis_index("member")
    taken = picks.shape[1]
    tile, width = halo.shape[1], halo.shape[2]
    offered = rows.shape[1] // tile
    each = stale_rows.shape[1] // tile
    depth = 512
    for p in range(members):
        for k in range(taken):
            asked[p, k] = jnp.broadcast_to(picks[p : p + 1, k : k + 1], asked.shape[2:])
    entered = greet(me_g, me_m, groups, members)
    wanted[me_m] = asked[me_m]
    bound[...] = pick_rows(rows[...], feats, depth).reshape(offered, tile, width)
    entered()
    copies, calls = [], []
    for o in range(1, members):
        peer = lax.rem(me_m + o, members)
        calls.append(
            push(asked.at[peer], wanted.at[me_m], p_send, p_recv, o, (me_g, peer))
        )

    def send_stale(o):
        to = lax.rem(me_g + o, groups)
        found = pick_rows(stale_rows[pl.ds(to, 1), :], hist, depth)
        found = found.astype(BF16).reshape(each, tile, width)
        at = pl.ds(me_g * each, each)
        if o == 0:
            stale[at] = found
        else:
            leaving[o] = found
            copies.append(push(leaving.at[o], stale.at[at], s_send, s_recv, o, (to, me_m)))

    def choose(p, k):
        w = jnp.broadcast_to(wanted[p, k][:1, :], (tile, width))
        value = bound[0]
        for j in range(1, offered):
            value = jnp.where(w == j, bound[j], value)
        return value.astype(BF16)

    for o in range(groups - 1, 1, -1):
        send_stale(o)
    for o in range(1, members):
        calls[o - 1].wait_recv()
        peer = lax.rem(me_m + members - o, members)
        for k in range(taken):
            outgoing[o, k] = choose(peer, k)
        at = pl.ds(me_m * taken, taken)
        copies.append(push(outgoing.at[o], halo.at[at], h_send, h_recv, o, (me_g, peer)))
    for k in range(taken):
        halo[me_m * taken + k] = choose(me_m, k)
    if groups > 1:
        send_stale(1)
    send_stale(0)
    for copy in calls:
        copy.wait_send()
    for copy in copies:
        copy.wait()


def gather(features, history, boundary_rows, picks, stale_rows, tile, groups, members):
    taken = picks.shape[1]
    width = features.shape[1]
    offered = boundary_rows.shape[1] // tile
    each = stale_rows.shape[1] // tile
    vmem = pl.BlockSpec(memory_space=pltpu.VMEM)
    dma = pltpu.SemaphoreType.DMA
    return pl.pallas_call(
        functools.partial(gather_kernel, groups, members),
        out_shape=(
            jax.ShapeDtypeStruct((members * taken, tile, width), BF16),
            jax.ShapeDtypeStruct((groups * each, tile, width), BF16),
            jax.ShapeDtypeStruct((members, taken, 8, 128), jnp.int32),
        ),
        in_specs=[vmem] * 5,
        out_specs=[vmem] * 3,
        scratch_shapes=[
            pltpu.VMEM((members, taken, 8, 128), jnp.int32),
            pltpu.VMEM((offered, tile, width), F32),
            pltpu.VMEM((members, taken, tile, width), BF16),
            pltpu.VMEM((groups, each, tile, width), BF16),
            dma((members,)),
            dma((members,)),
            dma((members,)),
            dma((members,)),
            dma((groups,)),
            dma((groups,)),
        ],
        compiler_params=pltpu.CompilerParams(
            collective_id=0, has_side_effects=True, vmem_limit_bytes=40 << 20
        ),
    )(features, history, boundary_rows, picks, stale_rows)


def combine_kernel(
    groups,
    members,
    factor,
    row_grad,
    halo_grad,
    part,
    wanted,
    rows,
    grad_features,
    g_self,
    g_neigh,
    returned,
    landed,
    partial,
    across,
    share,
    whole,
    h_send,
    h_recv,
    a_send,
    a_recv,
    b_send,
    b_recv,
    c_send,
    c_recv,
):
    me_g, me_m = lax.axis_index("group"), lax.axis_index("member")
    taken = wanted.shape[1]
    nodes, width = row_grad.shape
    tile = halo_grad.shape[1]
    offered = rows.shape[1] // tile
    piece = part.shape[0] // members
    greet(me_g, me_m, groups, members)()
    copies, first, second, third = [], [], [], []
    for o in range(1, members):
        peer = lax.rem(me_m + o, members)
        at = pl.ds(pl.multiple_of(peer * piece, piece), piece)
        first.append(
            push(part.at[at], landed.at[me_m], a_send, a_recv, o, (me_g, peer))
        )
    for o in range(1, members):
        peer = lax.rem(me_m + o, members)
        copies.append(
            push(
                halo_grad.at[pl.ds(peer * taken, taken)],
                returned.at[me_m],
                h_send,
                h_recv,
                o,
                (me_g, peer),
            )
        )
    landed[me_m] = part[pl.ds(pl.multiple_of(me_m * piece, piece), piece), :]
    returned[me_m] = halo_grad[pl.ds(me_m * taken, taken)]
    for copy in first:
        copy.wait_recv()
    total = landed[0]
    for p in range(1, members):
        total = total + landed[p]
    partial[...] = total
    across[me_g] = total
    for o in range(1, groups):
        to = lax.rem(me_g + o, groups)
        second.append(push(partial, across.at[me_g], b_send, b_recv, o, (to, me_m)))
    for copy in second:
        copy.wait_recv()
    total = across[0]
    for g in range(1, groups):
        total = total + across[g]
    mine = pl.ds(pl.multiple_of(me_m * piece, piece), piece)
    share[...] = total
    whole[mine, :] = total
    for o in range(1, members):
        peer = lax.rem(me_m + o, members)
        third.append(push(share, whole.at[mine], c_send, c_recv, o, (me_g, peer)))

    for copy in copies:
        copy.wait_recv()
    halves = []
    for j in range(offered):
        total = jnp.zeros((tile, width), F32)
        for p in range(members):
            for k in range(taken):
                w = jnp.broadcast_to(wanted[p, k][:1, :], (tile, width))
                total = total + jnp.where(w == j, returned[p, k].astype(F32), 0.0)
        high = total.astype(BF16)
        low = (total - high.astype(F32)).astype(BF16)
        halves.append(jnp.concatenate([high, low], axis=1))
    extra = jnp.concatenate(halves, axis=0)
    depth = 512

    def add(c):
        at = pl.ds(pl.multiple_of(c * depth, depth), depth)
        ids = lax.broadcasted_iota(jnp.int32, (depth, rows.shape[1]), 0) + c * depth
        hot = jnp.where(ids == rows[...], 1.0, 0.0).astype(BF16)
        more = jnp.dot(hot, extra, preferred_element_type=F32)
        grad_features[at, :] = (row_grad[at, :] + (more[:, :width] + more[:, width:])).astype(BF16)

    pl.loop(0, nodes // depth)(add)
    for copy in third:
        copy.wait_recv()
    g_self[...] = whole[:width, :] * factor
    g_neigh[...] = whole[width:, :] * factor
    for copy in first + second + third + copies:
        copy.wait_send()


def combine(row_grad, halo_grad, part, wanted, boundary_rows, groups, members, factor):
    nodes, width = row_grad.shape
    tile = halo_grad.shape[1]
    taken = wanted.shape[1]
    piece = part.shape[0] // members
    vmem = pl.BlockSpec(memory_space=pltpu.VMEM)
    dma = pltpu.SemaphoreType.DMA
    return pl.pallas_call(
        functools.partial(combine_kernel, groups, members, factor),
        out_shape=(
            jax.ShapeDtypeStruct((nodes, width), BF16),
            jax.ShapeDtypeStruct((width, part.shape[1]), F32),
            jax.ShapeDtypeStruct((width, part.shape[1]), F32),
        ),
        in_specs=[vmem] * 5,
        out_specs=[vmem] * 3,
        scratch_shapes=[
            pltpu.VMEM((members, taken, tile, width), BF16),
            pltpu.VMEM((members, piece, part.shape[1]), F32),
            pltpu.VMEM((piece, part.shape[1]), F32),
            pltpu.VMEM((groups, piece, part.shape[1]), F32),
            pltpu.VMEM((piece, part.shape[1]), F32),
            pltpu.VMEM(part.shape, F32),
            dma((members,)),
            dma((members,)),
            dma((members,)),
            dma((members,)),
            dma((groups,)),
            dma((groups,)),
            dma((members,)),
            dma((members,)),
        ],
        compiler_params=pltpu.CompilerParams(
            collective_id=1, has_side_effects=True, vmem_limit_bytes=40 << 20
        ),
    )(row_grad, halo_grad, part, wanted, boundary_rows)


def on_device(
    features,
    history,
    tiles,
    tile_src,
    degree,
    boundary_rows,
    picks,
    stale_rows,
    w_self,
    w_neigh,
    cotangent,
):
    members = lax.axis_size("member")
    groups = lax.axis_size("group")
    tile = tiles.shape[1]
    blocks = features.shape[0] // tile
    taken = picks.shape[1]
    plans = plan(tile_src, blocks + members * taken)
    halo, stale, wanted = gather(
        features, history, boundary_rows, picks, stale_rows, tile, groups, members
    )
    layer_out, row_grad, halo_grad, part = local(
        tile_src, plans, features, halo, stale, tiles, degree, w_self, w_neigh, cotangent
    )
    factor = 1.0 / math.sqrt(features.shape[0] * members * groups)
    grad_features, grad_self, grad_neigh = combine(
        row_grad, halo_grad, part, wanted, boundary_rows, groups, members, factor
    )
    return (layer_out, grad_features, grad_self, grad_neigh)


def solution(mesh):
    placed = (
        P(("group", "member"), None),
        P(("group", "member"), None),
        P(("group", "member"), None, None),
        P(("group", "member"), None),
        P(("group", "member")),
        P(("group", "member"), None),
        P(("group", "member"), None),
        P(("group", "member"), None),
        P(),
        P(),
        P(("group", "member"), None),
    )
    return jax.shard_map(
        on_device,
        mesh=mesh,
        in_specs=placed,
        out_specs=(P(("group", "member"), None), P(("group", "member"), None), P(), P()),
        check_vma=False,
    )
```

```python
import functools
import math

import jax
import jax.numpy as jnp
from jax import lax
from jax.experimental import pallas as pl
from jax.experimental.pallas import tpu as pltpu
from jax.sharding import PartitionSpec as P

QUAD = 4
STEP = 8
F32 = jnp.float32
BF16 = jnp.bfloat16
MESH = pl.DeviceIdType.MESH


def plan(tile_src, wanted_sources):
    flat = tile_src.reshape(-1)
    total = flat.shape[0]
    slots = (total + wanted_sources * (QUAD - 1)) // QUAD * QUAD
    slots = -(-slots // (QUAD * STEP)) * QUAD * STEP
    index = jnp.arange(total, dtype=jnp.int32)
    same = flat[:, None] == flat[None, :]
    within = jnp.sum(jnp.where(same & (index[None, :] < index[:, None]), 1, 0), axis=1)
    ids = jnp.arange(wanted_sources, dtype=jnp.int32)
    hit = flat[None, :] == ids[:, None]
    count = jnp.sum(hit.astype(jnp.int32), axis=1)
    padded = (count + QUAD - 1) // QUAD * QUAD
    offset = jnp.sum(jnp.where(ids[None, :] < ids[:, None], padded[None, :], 0), axis=1)
    base = jnp.sum(jnp.where(hit, offset[:, None], 0), axis=0)
    pos = jnp.where(flat < wanted_sources, base + within, -1)
    slot = jnp.arange(slots, dtype=jnp.int32)
    code = jnp.sum(jnp.where(pos[None, :] == slot[:, None], index[None, :] + 1, 0), axis=1)
    first = slot[::QUAD]
    inside = (offset[None, :] <= first[:, None]) & (first[:, None] < (offset + padded)[None, :])
    start = inside & (offset[None, :] == first[:, None])
    quad = jnp.sum(jnp.where(inside, 2 * ids[None, :], 0) + start.astype(jnp.int32), axis=1)
    end = jnp.sum(padded)
    quad = jnp.where(first < end, quad, 2 * wanted_sources + 1)
    used = ((end // QUAD + STEP - 1) // STEP).reshape(1)
    return code, quad, used


def local_kernel(
    src,
    code,
    quad,
    used,
    feats,
    halo,
    stale,
    tiles,
    deg,
    w_self,
    w_neigh,
    cot,
    out,
    row_grad,
    halo_grad,
    part,
    tbuf,
    srcs,
    agg,
    back,
    grad,
    gt,
    sems,
):
    blocks, per = src.shape
    tile, width = feats.shape[0] // blocks, feats.shape[1]
    n_halo, n_stale = halo.shape[0], stale.shape[0]

    def chunk(b):
        return pltpu.make_async_copy(
            tiles.at[pl.ds(b * per, per)], tbuf.at[pl.ds(b * per, per)], sems.at[b]
        )

    @pl.loop(0, blocks)
    def _(b):
        chunk(b).start()

    for b in range(blocks):
        srcs[b] = feats[b * tile : (b + 1) * tile, :]
    srcs[blocks : blocks + n_halo] = halo[...]
    srcs[blocks + n_halo :] = stale[...]
    grad[...] = jnp.zeros_like(grad)
    back[blocks] = jnp.zeros((width, tile), BF16)

    def forward(b):
        chunk(b).wait()
        lhs = jnp.concatenate([tbuf[b * per + t] for t in range(per)], axis=1)
        rhs = jnp.concatenate([srcs[src[b, t]] for t in range(per)], axis=0)
        total = jnp.dot(lhs, rhs, preferred_element_type=F32)
        d = jnp.broadcast_to(deg[pl.ds(b, 1), :].astype(F32), (tile, tile)).T
        agg[pl.ds(pl.multiple_of(b * tile, tile), tile), :] = (total / d).astype(BF16)

    pl.loop(0, blocks, unroll=2)(forward)

    gt[...] = jnp.zeros_like(gt)
    group = 8
    rows = group * tile
    w_cat = jnp.concatenate([w_self[...], w_neigh[...]], axis=0)

    def middle(c):
        at = pl.ds(pl.multiple_of(c * rows, rows), rows)
        fa = jnp.concatenate([feats[at, :], agg[at, :]], axis=1)
        pre = jnp.dot(fa, w_cat, preferred_element_type=F32)
        scale = lax.rsqrt(jnp.mean(pre * pre, axis=-1, keepdims=True) + 1e-05)
        out[at, :] = (pre * scale).astype(BF16)
        g = cot[at, :].astype(F32)
        m = jnp.mean(g * pre, axis=-1, keepdims=True)
        dpre = (scale * g - pre * (scale**3 * m)).astype(BF16)
        gt[...] += lax.dot_general(dpre, fa, (((0,), (0,)), ((), ())), preferred_element_type=F32)
        row_grad[at, :] = lax.dot_general(
            dpre, w_self[...], (((1,), (1,)), ((), ())), preferred_element_type=F32
        )
        bt = lax.dot_general(
            w_neigh[...], dpre, (((1,), (1,)), ((), ())), preferred_element_type=F32
        )
        for i in range(group):
            d = deg[pl.ds(c * group + i, 1), :].astype(F32)
            back[c * group + i] = (bt[:, i * tile : (i + 1) * tile] / d).astype(BF16)

    pl.loop(0, blocks // group)(middle)

    part[:width, :] = gt[:, :width].T
    part[width:, :] = gt[:, width:].T

    def backward(step, acc):
        terms = []
        for u in range(STEP):
            lhs, rhs = [], []
            for i in range(QUAD):
                k = code[(step * STEP + u) * QUAD + i]
                t = jnp.maximum(k - 1, 0)
                b = jnp.where(k == 0, blocks, t // per)
                lhs.append(back[b])
                rhs.append(tbuf[t])
            terms.append(
                jnp.dot(
                    jnp.concatenate(lhs, axis=1),
                    jnp.concatenate(rhs, axis=0),
                    preferred_element_type=F32,
                )
            )
        for u in range(STEP):
            info = quad[step * STEP + u]
            acc = terms[u] + jnp.where(info % 2 == 1, 0.0, acc)
            grad[info // 2] = acc
        return acc

    lax.fori_loop(0, used[0], backward, jnp.zeros((width, tile), F32))

    def finish(b):
        at = pl.ds(pl.multiple_of(b * tile, tile), tile)
        row_grad[at, :] += grad[b].T

    pl.loop(0, blocks, unroll=4)(finish)
    for h in range(n_halo):
        halo_grad[h] = grad[blocks + h].T.astype(BF16)


def local(tile_src, plans, features, halo, stale, tiles, degree, w_self, w_neigh, cotangent):
    blocks, per = tile_src.shape
    tile = tiles.shape[1]
    nodes, width = features.shape
    n_halo = halo.shape[0]
    smem = pl.BlockSpec(memory_space=pltpu.SMEM)
    vmem = pl.BlockSpec(memory_space=pltpu.VMEM)
    return pl.pallas_call(
        local_kernel,
        out_shape=(
            jax.ShapeDtypeStruct((nodes, width), BF16),
            jax.ShapeDtypeStruct((nodes, width), F32),
            jax.ShapeDtypeStruct((n_halo, tile, width), BF16),
            jax.ShapeDtypeStruct((2 * width, width), F32),
        ),
        in_specs=[smem] * 4
        + [vmem] * 3
        + [pl.BlockSpec(memory_space=pl.ANY)]
        + [vmem] * 4,
        out_specs=[vmem] * 4,
        scratch_shapes=[
            pltpu.VMEM(tiles.shape, BF16),
            pltpu.VMEM((blocks + n_halo + stale.shape[0], tile, width), BF16),
            pltpu.VMEM((nodes, width), BF16),
            pltpu.VMEM((blocks + 1, width, tile), BF16),
            pltpu.VMEM((blocks + n_halo + 1, width, tile), F32),
            pltpu.VMEM((width, 2 * width), F32),
            pltpu.SemaphoreType.DMA((blocks,)),
        ],
        compiler_params=pltpu.CompilerParams(vmem_limit_bytes=60 << 20),
    )(
        tile_src,
        *plans,
        features,
        halo,
        stale,
        tiles,
        degree.reshape(blocks, tile),
        w_self,
        w_neigh,
        cotangent,
    )


def greet(me_g, me_m, groups, members):
    barrier = pltpu.get_barrier_semaphore()
    for o in range(1, members):
        pl.semaphore_signal(
            barrier, inc=1, device_id=(me_g, lax.rem(me_m + o, members)), device_id_type=MESH
        )
    for o in range(1, groups):
        pl.semaphore_signal(
            barrier, inc=1, device_id=(lax.rem(me_g + o, groups), me_m), device_id_type=MESH
        )
    return lambda: pl.semaphore_wait(barrier, members + groups - 2)


def push(src, dst, send, recv, o, device):
    copy = pltpu.make_async_remote_copy(
        src_ref=src,
        dst_ref=dst,
        send_sem=send.at[o],
        recv_sem=recv.at[o],
        device_id=device,
        device_id_type=MESH,
    )
    copy.start()
    return copy


def pick_rows(row, table, depth):
    count = row.shape[1]
    column = jnp.broadcast_to(row, (8, count)).T[:, :1]
    total = jnp.zeros((count, table.shape[1]), F32)
    for c in range(0, table.shape[0], depth):
        ids = lax.broadcasted_iota(jnp.int32, (count, depth), 1) + c
        hot = jnp.where(ids == column, 1.0, 0.0).astype(BF16)
        total = total + jnp.dot(hot, table[c : c + depth, :], preferred_element_type=F32)
    return total


def gather_kernel(
    groups,
    members,
    feats_in,
    hist_in,
    rows,
    picks,
    stale_rows,
    halo,
    stale,
    wanted,
    asked,
    feats,
    hist,
    bound,
    outgoing,
    leaving,
    l_sems,
    p_send,
    p_recv,
    h_send,
    h_recv,
    s_send,
    s_recv,
):
    me_g, me_m = lax.axis_index("group"), lax.axis_index("member")
    taken = picks.shape[1]
    tile, width = halo.shape[1], halo.shape[2]
    offered = rows.shape[1] // tile
    each = stale_rows.shape[1] // tile
    depth = 512
    load_feats = pltpu.make_async_copy(feats_in, feats, l_sems.at[0])
    load_hist = pltpu.make_async_copy(hist_in, hist, l_sems.at[1])
    load_feats.start()
    load_hist.start()
    for p in range(members):
        for k in range(taken):
            asked[p, k] = jnp.broadcast_to(picks[p : p + 1, k : k + 1], asked.shape[2:])
    entered = greet(me_g, me_m, groups, members)
    wanted[me_m] = asked[me_m]
    load_feats.wait()
    bound[...] = pick_rows(rows[...], feats, depth).reshape(offered, tile, width)
    entered()
    load_hist.wait()
    copies, calls = [], []
    for o in range(1, members):
        peer = lax.rem(me_m + o, members)
        calls.append(
            push(asked.at[peer], wanted.at[me_m], p_send, p_recv, o, (me_g, peer))
        )

    def send_stale(o):
        to = lax.rem(me_g + o, groups)
        found = pick_rows(stale_rows[pl.ds(to, 1), :], hist, depth)
        found = found.astype(BF16).reshape(each, tile, width)
        at = pl.ds(me_g * each, each)
        if o == 0:
            stale[at] = found
        else:
            leaving[o] = found
            copies.append(push(leaving.at[o], stale.at[at], s_send, s_recv, o, (to, me_m)))

    def choose(p, k):
        w = jnp.broadcast_to(wanted[p, k][:1, :], (tile, width))
        value = bound[0]
        for j in range(1, offered):
            value = jnp.where(w == j, bound[j], value)
        return value.astype(BF16)

    for o in range(groups - 1, 1, -1):
        send_stale(o)
    for o in range(1, members):
        calls[o - 1].wait_recv()
        peer = lax.rem(me_m + members - o, members)
        for k in range(taken):
            outgoing[o, k] = choose(peer, k)
        at = pl.ds(me_m * taken, taken)
        copies.append(push(outgoing.at[o], halo.at[at], h_send, h_recv, o, (me_g, peer)))
    for k in range(taken):
        halo[me_m * taken + k] = choose(me_m, k)
    if groups > 1:
        send_stale(1)
    send_stale(0)
    for copy in calls:
        copy.wait_send()
    for copy in copies:
        copy.wait()


def gather(features, history, boundary_rows, picks, stale_rows, tile, groups, members):
    taken = picks.shape[1]
    width = features.shape[1]
    offered = boundary_rows.shape[1] // tile
    each = stale_rows.shape[1] // tile
    vmem = pl.BlockSpec(memory_space=pltpu.VMEM)
    dma = pltpu.SemaphoreType.DMA
    return pl.pallas_call(
        functools.partial(gather_kernel, groups, members),
        out_shape=(
            jax.ShapeDtypeStruct((members * taken, tile, width), BF16),
            jax.ShapeDtypeStruct((groups * each, tile, width), BF16),
            jax.ShapeDtypeStruct((members, taken, 8, 128), jnp.int32),
        ),
        in_specs=[pl.BlockSpec(memory_space=pl.ANY)] * 2 + [vmem] * 3,
        out_specs=[vmem] * 3,
        scratch_shapes=[
            pltpu.VMEM((members, taken, 8, 128), jnp.int32),
            pltpu.VMEM(features.shape, BF16),
            pltpu.VMEM(history.shape, BF16),
            pltpu.VMEM((offered, tile, width), F32),
            pltpu.VMEM((members, taken, tile, width), BF16),
            pltpu.VMEM((groups, each, tile, width), BF16),
            dma((2,)),
            dma((members,)),
            dma((members,)),
            dma((members,)),
            dma((members,)),
            dma((groups,)),
            dma((groups,)),
        ],
        compiler_params=pltpu.CompilerParams(
            collective_id=0, has_side_effects=True, vmem_limit_bytes=60 << 20
        ),
    )(features, history, boundary_rows, picks, stale_rows)


def combine_kernel(
    groups,
    members,
    factor,
    row_grad_in,
    halo_grad,
    part,
    wanted,
    rows,
    grad_features,
    g_self,
    g_neigh,
    row_grad,
    l_sem,
    returned,
    landed,
    partial,
    across,
    share,
    whole,
    h_send,
    h_recv,
    a_send,
    a_recv,
    b_send,
    b_recv,
    c_send,
    c_recv,
):
    me_g, me_m = lax.axis_index("group"), lax.axis_index("member")
    taken = wanted.shape[1]
    nodes, width = row_grad.shape
    tile = halo_grad.shape[1]
    offered = rows.shape[1] // tile
    piece = part.shape[0] // members
    load = pltpu.make_async_copy(row_grad_in, row_grad, l_sem)
    load.start()
    greet(me_g, me_m, groups, members)()
    copies, first, second, third = [], [], [], []
    for o in range(1, members):
        peer = lax.rem(me_m + o, members)
        at = pl.ds(pl.multiple_of(peer * piece, piece), piece)
        first.append(
            push(part.at[at], landed.at[me_m], a_send, a_recv, o, (me_g, peer))
        )
    for o in range(1, members):
        peer = lax.rem(me_m + o, members)
        copies.append(
            push(
                halo_grad.at[pl.ds(peer * taken, taken)],
                returned.at[me_m],
                h_send,
                h_recv,
                o,
                (me_g, peer),
            )
        )
    landed[me_m] = part[pl.ds(pl.multiple_of(me_m * piece, piece), piece), :]
    returned[me_m] = halo_grad[pl.ds(me_m * taken, taken)]
    for copy in first:
        copy.wait_recv()
    total = landed[0]
    for p in range(1, members):
        total = total + landed[p]
    partial[...] = total
    across[me_g] = total
    for o in range(1, groups):
        to = lax.rem(me_g + o, groups)
        second.append(push(partial, across.at[me_g], b_send, b_recv, o, (to, me_m)))
    for copy in second:
        copy.wait_recv()
    total = across[0]
    for g in range(1, groups):
        total = total + across[g]
    mine = pl.ds(pl.multiple_of(me_m * piece, piece), piece)
    share[...] = total
    whole[mine, :] = total
    for o in range(1, members):
        peer = lax.rem(me_m + o, members)
        third.append(push(share, whole.at[mine], c_send, c_recv, o, (me_g, peer)))

    for copy in copies:
        copy.wait_recv()
    halves = []
    for j in range(offered):
        total = jnp.zeros((tile, width), F32)
        for p in range(members):
            for k in range(taken):
                w = jnp.broadcast_to(wanted[p, k][:1, :], (tile, width))
                total = total + jnp.where(w == j, returned[p, k].astype(F32), 0.0)
        high = total.astype(BF16)
        low = (total - high.astype(F32)).astype(BF16)
        halves.append(jnp.concatenate([high, low], axis=1))
    extra = jnp.concatenate(halves, axis=0)
    load.wait()
    depth = 512

    def add(c):
        at = pl.ds(pl.multiple_of(c * depth, depth), depth)
        ids = lax.broadcasted_iota(jnp.int32, (depth, rows.shape[1]), 0) + c * depth
        hot = jnp.where(ids == rows[...], 1.0, 0.0).astype(BF16)
        more = jnp.dot(hot, extra, preferred_element_type=F32)
        grad_features[at, :] = (row_grad[at, :] + (more[:, :width] + more[:, width:])).astype(BF16)

    pl.loop(0, nodes // depth)(add)
    for copy in third:
        copy.wait_recv()
    g_self[...] = whole[:width, :] * factor
    g_neigh[...] = whole[width:, :] * factor
    for copy in first + second + third + copies:
        copy.wait_send()


def combine(row_grad, halo_grad, part, wanted, boundary_rows, groups, members, factor):
    nodes, width = row_grad.shape
    tile = halo_grad.shape[1]
    taken = wanted.shape[1]
    piece = part.shape[0] // members
    vmem = pl.BlockSpec(memory_space=pltpu.VMEM)
    dma = pltpu.SemaphoreType.DMA
    return pl.pallas_call(
        functools.partial(combine_kernel, groups, members, factor),
        out_shape=(
            jax.ShapeDtypeStruct((nodes, width), BF16),
            jax.ShapeDtypeStruct((width, part.shape[1]), F32),
            jax.ShapeDtypeStruct((width, part.shape[1]), F32),
        ),
        in_specs=[pl.BlockSpec(memory_space=pl.ANY)] + [vmem] * 4,
        out_specs=[vmem] * 3,
        scratch_shapes=[
            pltpu.VMEM((nodes, width), F32),
            dma(()),
            pltpu.VMEM((members, taken, tile, width), BF16),
            pltpu.VMEM((members, piece, part.shape[1]), F32),
            pltpu.VMEM((piece, part.shape[1]), F32),
            pltpu.VMEM((groups, piece, part.shape[1]), F32),
            pltpu.VMEM((piece, part.shape[1]), F32),
            pltpu.VMEM(part.shape, F32),
            dma((members,)),
            dma((members,)),
            dma((members,)),
            dma((members,)),
            dma((groups,)),
            dma((groups,)),
            dma((members,)),
            dma((members,)),
        ],
        compiler_params=pltpu.CompilerParams(
            collective_id=1, has_side_effects=True, vmem_limit_bytes=60 << 20
        ),
    )(row_grad, halo_grad, part, wanted, boundary_rows)


def on_device(
    features,
    history,
    tiles,
    tile_src,
    degree,
    boundary_rows,
    picks,
    stale_rows,
    w_self,
    w_neigh,
    cotangent,
):
    members = lax.axis_size("member")
    groups = lax.axis_size("group")
    tile = tiles.shape[1]
    blocks = features.shape[0] // tile
    taken = picks.shape[1]
    plans = plan(tile_src, blocks + members * taken)
    halo, stale, wanted = gather(
        features, history, boundary_rows, picks, stale_rows, tile, groups, members
    )
    layer_out, row_grad, halo_grad, part = local(
        tile_src, plans, features, halo, stale, tiles, degree, w_self, w_neigh, cotangent
    )
    factor = 1.0 / math.sqrt(features.shape[0] * members * groups)
    grad_features, grad_self, grad_neigh = combine(
        row_grad, halo_grad, part, wanted, boundary_rows, groups, members, factor
    )
    return (layer_out, grad_features, grad_self, grad_neigh)


def solution(mesh):
    placed = (
        P(("group", "member"), None),
        P(("group", "member"), None),
        P(("group", "member"), None, None),
        P(("group", "member"), None),
        P(("group", "member")),
        P(("group", "member"), None),
        P(("group", "member"), None),
        P(("group", "member"), None),
        P(),
        P(),
        P(("group", "member"), None),
    )
    return jax.shard_map(
        on_device,
        mesh=mesh,
        in_specs=placed,
        out_specs=(P(("group", "member"), None), P(("group", "member"), None), P(), P()),
        check_vma=False,
    )
```

```python
import functools
import math

import jax
import jax.numpy as jnp
from jax import lax
from jax.experimental import pallas as pl
from jax.experimental.pallas import tpu as pltpu
from jax.sharding import PartitionSpec as P

QUAD = 4
STEP = 8
F32 = jnp.float32
BF16 = jnp.bfloat16
MESH = pl.DeviceIdType.MESH


def plan_sizes(total, wanted_sources):
    slots = total + wanted_sources * (QUAD - 1)
    slots = -(-slots // 128) * 128
    return slots, -(-(slots // QUAD) // 128) * 128


def plan(row, wanted_sources, slots, quads):
    total = row.shape[1]
    wide = -(-wanted_sources // 128) * 128

    def iota(shape, axis):
        return lax.broadcasted_iota(jnp.int32, shape, axis).astype(F32)

    def column(value):
        return jnp.broadcast_to(value, (8, value.shape[1])).T[:, :1]

    row = row.astype(F32)
    square = (total, total)
    same = (column(row) == row) & (iota(square, 0) < iota(square, 1))
    within = jnp.sum(jnp.where(same, 1.0, 0.0), axis=0, keepdims=True)
    ids = iota((wide, total), 0)
    hit = (ids == row) & (ids < wanted_sources)
    count = jnp.sum(jnp.where(hit, 1.0, 0.0), axis=1, keepdims=True)
    need = jnp.floor((count + (QUAD - 1)) / QUAD)
    spread = jnp.broadcast_to(need, (wide, wide)).T
    before = iota((wide, wide), 1) < iota((wide, wide), 0)
    offset = jnp.sum(jnp.where(before, spread, 0.0), axis=1, keepdims=True)
    end = jnp.sum(spread[:1, :], axis=1, keepdims=True)
    base = jnp.sum(jnp.where(hit, QUAD * offset, 0.0), axis=0, keepdims=True)
    pos = jnp.where(row < wanted_sources, base + within, -1.0)
    here = column(pos) == iota((total, slots), 1)
    code = jnp.sum(jnp.where(here, iota((total, slots), 0) + 1.0, 0.0), axis=0, keepdims=True)
    q = iota((wide, quads), 1)
    inside = (offset <= q) & (q < offset + need)
    info = 2.0 * iota((wide, quads), 0) + jnp.where(offset == q, 1.0, 0.0)
    quad = jnp.sum(jnp.where(inside, info, 0.0), axis=0, keepdims=True)
    quad = jnp.where(q[:1, :] < end, quad, 2.0 * wanted_sources + 1.0)
    used = jnp.broadcast_to(jnp.floor((end + (STEP - 1)) / STEP), (1, 128))
    return code.astype(jnp.int32), quad.astype(jnp.int32), used.astype(jnp.int32)


def local_kernel(
    src,
    code,
    quad,
    used,
    feats,
    halo,
    stale,
    tiles,
    deg,
    w_self,
    w_neigh,
    cot,
    out,
    row_grad,
    halo_grad,
    part,
    tbuf,
    srcs,
    agg,
    back,
    grad,
    gt,
    sems,
):
    blocks = deg.shape[0]
    per = src.shape[1] // blocks
    tile, width = feats.shape[0] // blocks, feats.shape[1]
    n_halo, n_stale = halo.shape[0], stale.shape[0]

    def chunk(b):
        return pltpu.make_async_copy(
            tiles.at[pl.ds(b * per, per)], tbuf.at[pl.ds(b * per, per)], sems.at[b]
        )

    @pl.loop(0, blocks)
    def _(b):
        chunk(b).start()

    for b in range(blocks):
        srcs[b] = feats[b * tile : (b + 1) * tile, :]
    srcs[blocks : blocks + n_halo] = halo[...]
    srcs[blocks + n_halo :] = stale[...]
    grad[...] = jnp.zeros_like(grad)
    back[blocks] = jnp.zeros((width, tile), BF16)

    def forward(b):
        chunk(b).wait()
        lhs = jnp.concatenate([tbuf[b * per + t] for t in range(per)], axis=1)
        rhs = jnp.concatenate([srcs[src[0, b * per + t]] for t in range(per)], axis=0)
        total = jnp.dot(lhs, rhs, preferred_element_type=F32)
        d = jnp.broadcast_to(deg[pl.ds(b, 1), :].astype(F32), (tile, tile)).T
        agg[pl.ds(pl.multiple_of(b * tile, tile), tile), :] = (total / d).astype(BF16)

    pl.loop(0, blocks, unroll=2)(forward)

    gt[...] = jnp.zeros_like(gt)
    group = 8
    rows = group * tile
    w_cat = jnp.concatenate([w_self[...], w_neigh[...]], axis=0)

    def middle(c):
        at = pl.ds(pl.multiple_of(c * rows, rows), rows)
        fa = jnp.concatenate([feats[at, :], agg[at, :]], axis=1)
        pre = jnp.dot(fa, w_cat, preferred_element_type=F32)
        scale = lax.rsqrt(jnp.mean(pre * pre, axis=-1, keepdims=True) + 1e-05)
        out[at, :] = (pre * scale).astype(BF16)
        g = cot[at, :].astype(F32)
        m = jnp.mean(g * pre, axis=-1, keepdims=True)
        dpre = (scale * g - pre * (scale**3 * m)).astype(BF16)
        gt[...] += lax.dot_general(dpre, fa, (((0,), (0,)), ((), ())), preferred_element_type=F32)
        row_grad[at, :] = lax.dot_general(
            dpre, w_self[...], (((1,), (1,)), ((), ())), preferred_element_type=F32
        )
        bt = lax.dot_general(
            w_neigh[...], dpre, (((1,), (1,)), ((), ())), preferred_element_type=F32
        )
        for i in range(group):
            d = deg[pl.ds(c * group + i, 1), :].astype(F32)
            back[c * group + i] = (bt[:, i * tile : (i + 1) * tile] / d).astype(BF16)

    pl.loop(0, blocks // group)(middle)

    part[:width, :] = gt[:, :width].T
    part[width:, :] = gt[:, width:].T

    def backward(step, acc):
        terms = []
        for u in range(STEP):
            lhs, rhs = [], []
            for i in range(QUAD):
                k = code[0, (step * STEP + u) * QUAD + i]
                t = jnp.maximum(k - 1, 0)
                b = jnp.where(k == 0, blocks, t // per)
                lhs.append(back[b])
                rhs.append(tbuf[t])
            terms.append(
                jnp.dot(
                    jnp.concatenate(lhs, axis=1),
                    jnp.concatenate(rhs, axis=0),
                    preferred_element_type=F32,
                )
            )
        for u in range(STEP):
            info = quad[0, step * STEP + u]
            acc = terms[u] + jnp.where(info % 2 == 1, 0.0, acc)
            grad[info // 2] = acc
        return acc

    lax.fori_loop(0, used[0, 0], backward, jnp.zeros((width, tile), F32))

    def finish(b):
        at = pl.ds(pl.multiple_of(b * tile, tile), tile)
        row_grad[at, :] += grad[b].T

    pl.loop(0, blocks, unroll=4)(finish)
    for h in range(n_halo):
        halo_grad[h] = grad[blocks + h].T.astype(BF16)


def local(tile_src, plans, features, halo, stale, tiles, degree, w_self, w_neigh, cotangent):
    tile = tiles.shape[1]
    nodes, width = features.shape
    blocks = nodes // tile
    n_halo = halo.shape[0]
    smem = pl.BlockSpec(memory_space=pltpu.SMEM)
    vmem = pl.BlockSpec(memory_space=pltpu.VMEM)
    return pl.pallas_call(
        local_kernel,
        out_shape=(
            jax.ShapeDtypeStruct((nodes, width), BF16),
            jax.ShapeDtypeStruct((nodes, width), F32),
            jax.ShapeDtypeStruct((n_halo, tile, width), BF16),
            jax.ShapeDtypeStruct((2 * width, width), F32),
        ),
        in_specs=[smem] * 4
        + [vmem] * 3
        + [pl.BlockSpec(memory_space=pl.ANY)]
        + [vmem] * 4,
        out_specs=[vmem] * 4,
        scratch_shapes=[
            pltpu.VMEM(tiles.shape, BF16),
            pltpu.VMEM((blocks + n_halo + stale.shape[0], tile, width), BF16),
            pltpu.VMEM((nodes, width), BF16),
            pltpu.VMEM((blocks + 1, width, tile), BF16),
            pltpu.VMEM((blocks + n_halo + 1, width, tile), F32),
            pltpu.VMEM((width, 2 * width), F32),
            pltpu.SemaphoreType.DMA((blocks,)),
        ],
        compiler_params=pltpu.CompilerParams(vmem_limit_bytes=60 << 20),
    )(
        tile_src,
        *plans,
        features,
        halo,
        stale,
        tiles,
        degree.reshape(blocks, tile),
        w_self,
        w_neigh,
        cotangent,
    )


def greet(me_g, me_m, groups, members):
    barrier = pltpu.get_barrier_semaphore()
    for o in range(1, members):
        pl.semaphore_signal(
            barrier, inc=1, device_id=(me_g, lax.rem(me_m + o, members)), device_id_type=MESH
        )
    for o in range(1, groups):
        pl.semaphore_signal(
            barrier, inc=1, device_id=(lax.rem(me_g + o, groups), me_m), device_id_type=MESH
        )
    return lambda: pl.semaphore_wait(barrier, members + groups - 2)


def push(src, dst, send, recv, o, device):
    copy = pltpu.make_async_remote_copy(
        src_ref=src,
        dst_ref=dst,
        send_sem=send.at[o],
        recv_sem=recv.at[o],
        device_id=device,
        device_id_type=MESH,
    )
    copy.start()
    return copy


def pick_rows(row, table, depth):
    count = row.shape[1]
    column = jnp.broadcast_to(row, (8, count)).T[:, :1]
    total = jnp.zeros((count, table.shape[1]), F32)
    for c in range(0, table.shape[0], depth):
        ids = lax.broadcasted_iota(jnp.int32, (count, depth), 1) + c
        hot = jnp.where(ids == column, 1.0, 0.0).astype(BF16)
        total = total + jnp.dot(hot, table[c : c + depth, :], preferred_element_type=F32)
    return total


def gather_kernel(
    groups,
    members,
    feats_in,
    hist_in,
    rows,
    picks,
    stale_rows,
    tile_src,
    halo,
    stale,
    wanted,
    code,
    quad,
    used,
    asked,
    feats,
    hist,
    bound,
    outgoing,
    leaving,
    l_sems,
    p_send,
    p_recv,
    h_send,
    h_recv,
    s_send,
    s_recv,
):
    me_g, me_m = lax.axis_index("group"), lax.axis_index("member")
    taken = picks.shape[1]
    tile, width = halo.shape[1], halo.shape[2]
    offered = rows.shape[1] // tile
    each = stale_rows.shape[1] // tile
    depth = 512
    load_feats = pltpu.make_async_copy(feats_in, feats, l_sems.at[0])
    load_hist = pltpu.make_async_copy(hist_in, hist, l_sems.at[1])
    load_feats.start()
    load_hist.start()
    for p in range(members):
        for k in range(taken):
            asked[p, k] = jnp.broadcast_to(picks[p : p + 1, k : k + 1], asked.shape[2:])
    entered = greet(me_g, me_m, groups, members)
    wanted[me_m] = asked[me_m]
    load_feats.wait()
    bound[...] = pick_rows(rows[...], feats, depth).reshape(offered, tile, width)
    entered()
    load_hist.wait()
    copies, calls = [], []
    for o in range(1, members):
        peer = lax.rem(me_m + o, members)
        calls.append(
            push(asked.at[peer], wanted.at[me_m], p_send, p_recv, o, (me_g, peer))
        )

    def send_stale(o):
        to = lax.rem(me_g + o, groups)
        found = pick_rows(stale_rows[pl.ds(to, 1), :], hist, depth)
        found = found.astype(BF16).reshape(each, tile, width)
        at = pl.ds(me_g * each, each)
        if o == 0:
            stale[at] = found
        else:
            leaving[o] = found
            copies.append(push(leaving.at[o], stale.at[at], s_send, s_recv, o, (to, me_m)))

    def choose(p, k):
        w = jnp.broadcast_to(wanted[p, k][:1, :], (tile, width))
        value = bound[0]
        for j in range(1, offered):
            value = jnp.where(w == j, bound[j], value)
        return value.astype(BF16)

    for o in range(groups - 1, 1, -1):
        send_stale(o)
    for o in range(1, members):
        calls[o - 1].wait_recv()
        peer = lax.rem(me_m + members - o, members)
        for k in range(taken):
            outgoing[o, k] = choose(peer, k)
        at = pl.ds(me_m * taken, taken)
        copies.append(push(outgoing.at[o], halo.at[at], h_send, h_recv, o, (me_g, peer)))
    for k in range(taken):
        halo[me_m * taken + k] = choose(me_m, k)
    if groups > 1:
        send_stale(1)
    send_stale(0)
    blocks = feats.shape[0] // tile
    code[...], quad[...], used[...] = plan(
        tile_src[...], blocks + members * taken, code.shape[1], quad.shape[1]
    )
    for copy in calls:
        copy.wait_send()
    for copy in copies:
        copy.wait()


def gather(features, history, boundary_rows, picks, stale_rows, tile_src, tile, groups, members):
    taken = picks.shape[1]
    width = features.shape[1]
    offered = boundary_rows.shape[1] // tile
    each = stale_rows.shape[1] // tile
    wanted_sources = features.shape[0] // tile + members * taken
    slots, quads = plan_sizes(tile_src.shape[1], wanted_sources)
    vmem = pl.BlockSpec(memory_space=pltpu.VMEM)
    dma = pltpu.SemaphoreType.DMA
    return pl.pallas_call(
        functools.partial(gather_kernel, groups, members),
        out_shape=(
            jax.ShapeDtypeStruct((members * taken, tile, width), BF16),
            jax.ShapeDtypeStruct((groups * each, tile, width), BF16),
            jax.ShapeDtypeStruct((members, taken, 8, 128), jnp.int32),
            jax.ShapeDtypeStruct((1, slots), jnp.int32),
            jax.ShapeDtypeStruct((1, quads), jnp.int32),
            jax.ShapeDtypeStruct((1, 128), jnp.int32),
        ),
        in_specs=[pl.BlockSpec(memory_space=pl.ANY)] * 2 + [vmem] * 4,
        out_specs=[vmem] * 6,
        scratch_shapes=[
            pltpu.VMEM((members, taken, 8, 128), jnp.int32),
            pltpu.VMEM(features.shape, BF16),
            pltpu.VMEM(history.shape, BF16),
            pltpu.VMEM((offered, tile, width), F32),
            pltpu.VMEM((members, taken, tile, width), BF16),
            pltpu.VMEM((groups, each, tile, width), BF16),
            dma((2,)),
            dma((members,)),
            dma((members,)),
            dma((members,)),
            dma((members,)),
            dma((groups,)),
            dma((groups,)),
        ],
        compiler_params=pltpu.CompilerParams(
            collective_id=0, has_side_effects=True, vmem_limit_bytes=60 << 20
        ),
    )(features, history, boundary_rows, picks, stale_rows, tile_src)


def combine_kernel(
    groups,
    members,
    factor,
    row_grad_in,
    halo_grad,
    part,
    wanted,
    rows,
    grad_features,
    g_self,
    g_neigh,
    row_grad,
    l_sem,
    returned,
    landed,
    partial,
    across,
    share,
    whole,
    h_send,
    h_recv,
    a_send,
    a_recv,
    b_send,
    b_recv,
    c_send,
    c_recv,
):
    me_g, me_m = lax.axis_index("group"), lax.axis_index("member")
    taken = wanted.shape[1]
    nodes, width = row_grad.shape
    tile = halo_grad.shape[1]
    offered = rows.shape[1] // tile
    piece = part.shape[0] // members
    load = pltpu.make_async_copy(row_grad_in, row_grad, l_sem)
    load.start()
    greet(me_g, me_m, groups, members)()
    copies, first, second, third = [], [], [], []
    for o in range(1, members):
        peer = lax.rem(me_m + o, members)
        at = pl.ds(pl.multiple_of(peer * piece, piece), piece)
        first.append(
            push(part.at[at], landed.at[me_m], a_send, a_recv, o, (me_g, peer))
        )
    for o in range(1, members):
        peer = lax.rem(me_m + o, members)
        copies.append(
            push(
                halo_grad.at[pl.ds(peer * taken, taken)],
                returned.at[me_m],
                h_send,
                h_recv,
                o,
                (me_g, peer),
            )
        )
    landed[me_m] = part[pl.ds(pl.multiple_of(me_m * piece, piece), piece), :]
    returned[me_m] = halo_grad[pl.ds(me_m * taken, taken)]
    for copy in first:
        copy.wait_recv()
    total = landed[0]
    for p in range(1, members):
        total = total + landed[p]
    partial[...] = total
    across[me_g] = total
    for o in range(1, groups):
        to = lax.rem(me_g + o, groups)
        second.append(push(partial, across.at[me_g], b_send, b_recv, o, (to, me_m)))
    for copy in second:
        copy.wait_recv()
    total = across[0]
    for g in range(1, groups):
        total = total + across[g]
    mine = pl.ds(pl.multiple_of(me_m * piece, piece), piece)
    share[...] = total
    whole[mine, :] = total
    for o in range(1, members):
        peer = lax.rem(me_m + o, members)
        third.append(push(share, whole.at[mine], c_send, c_recv, o, (me_g, peer)))

    for copy in copies:
        copy.wait_recv()
    halves = []
    for j in range(offered):
        total = jnp.zeros((tile, width), F32)
        for p in range(members):
            for k in range(taken):
                w = jnp.broadcast_to(wanted[p, k][:1, :], (tile, width))
                total = total + jnp.where(w == j, returned[p, k].astype(F32), 0.0)
        high = total.astype(BF16)
        low = (total - high.astype(F32)).astype(BF16)
        halves.append(jnp.concatenate([high, low], axis=1))
    extra = jnp.concatenate(halves, axis=0)
    load.wait()
    depth = 512

    def add(c):
        at = pl.ds(pl.multiple_of(c * depth, depth), depth)
        ids = lax.broadcasted_iota(jnp.int32, (depth, rows.shape[1]), 0) + c * depth
        hot = jnp.where(ids == rows[...], 1.0, 0.0).astype(BF16)
        more = jnp.dot(hot, extra, preferred_element_type=F32)
        grad_features[at, :] = (row_grad[at, :] + (more[:, :width] + more[:, width:])).astype(BF16)

    pl.loop(0, nodes // depth)(add)
    for copy in third:
        copy.wait_recv()
    g_self[...] = whole[:width, :] * factor
    g_neigh[...] = whole[width:, :] * factor
    for copy in first + second + third + copies:
        copy.wait_send()


def combine(row_grad, halo_grad, part, wanted, boundary_rows, groups, members, factor):
    nodes, width = row_grad.shape
    tile = halo_grad.shape[1]
    taken = wanted.shape[1]
    piece = part.shape[0] // members
    vmem = pl.BlockSpec(memory_space=pltpu.VMEM)
    dma = pltpu.SemaphoreType.DMA
    return pl.pallas_call(
        functools.partial(combine_kernel, groups, members, factor),
        out_shape=(
            jax.ShapeDtypeStruct((nodes, width), BF16),
            jax.ShapeDtypeStruct((width, part.shape[1]), F32),
            jax.ShapeDtypeStruct((width, part.shape[1]), F32),
        ),
        in_specs=[pl.BlockSpec(memory_space=pl.ANY)] + [vmem] * 4,
        out_specs=[vmem] * 3,
        scratch_shapes=[
            pltpu.VMEM((nodes, width), F32),
            dma(()),
            pltpu.VMEM((members, taken, tile, width), BF16),
            pltpu.VMEM((members, piece, part.shape[1]), F32),
            pltpu.VMEM((piece, part.shape[1]), F32),
            pltpu.VMEM((groups, piece, part.shape[1]), F32),
            pltpu.VMEM((piece, part.shape[1]), F32),
            pltpu.VMEM(part.shape, F32),
            dma((members,)),
            dma((members,)),
            dma((members,)),
            dma((members,)),
            dma((groups,)),
            dma((groups,)),
            dma((members,)),
            dma((members,)),
        ],
        compiler_params=pltpu.CompilerParams(
            collective_id=1, has_side_effects=True, vmem_limit_bytes=60 << 20
        ),
    )(row_grad, halo_grad, part, wanted, boundary_rows)


def on_device(
    features,
    history,
    tiles,
    tile_src,
    degree,
    boundary_rows,
    picks,
    stale_rows,
    w_self,
    w_neigh,
    cotangent,
):
    members = lax.axis_size("member")
    groups = lax.axis_size("group")
    tile = tiles.shape[1]
    tile_src = tile_src.reshape(1, -1)
    halo, stale, wanted, *plans = gather(
        features, history, boundary_rows, picks, stale_rows, tile_src, tile, groups, members
    )
    layer_out, row_grad, halo_grad, part = local(
        tile_src, plans, features, halo, stale, tiles, degree, w_self, w_neigh, cotangent
    )
    factor = 1.0 / math.sqrt(features.shape[0] * members * groups)
    grad_features, grad_self, grad_neigh = combine(
        row_grad, halo_grad, part, wanted, boundary_rows, groups, members, factor
    )
    return (layer_out, grad_features, grad_self, grad_neigh)


def solution(mesh):
    placed = (
        P(("group", "member"), None),
        P(("group", "member"), None),
        P(("group", "member"), None, None),
        P(("group", "member"), None),
        P(("group", "member")),
        P(("group", "member"), None),
        P(("group", "member"), None),
        P(("group", "member"), None),
        P(),
        P(),
        P(("group", "member"), None),
    )
    return jax.shard_map(
        on_device,
        mesh=mesh,
        in_specs=placed,
        out_specs=(P(("group", "member"), None), P(("group", "member"), None), P(), P()),
        check_vma=False,
    )
```

```python
import functools
import math

import jax
import jax.numpy as jnp
from jax import lax
from jax.experimental import pallas as pl
from jax.experimental.pallas import tpu as pltpu
from jax.sharding import PartitionSpec as P

QUAD = 4
STEP = 8
F32 = jnp.float32
BF16 = jnp.bfloat16
MESH = pl.DeviceIdType.MESH


def plan_sizes(total, wanted_sources):
    slots = total + wanted_sources * (QUAD - 1)
    slots = -(-slots // 128) * 128
    return slots, -(-(slots // QUAD) // 128) * 128


def plan(row, wanted_sources, slots, quads):
    total = row.shape[1]
    wide = -(-wanted_sources // 128) * 128

    def iota(shape, axis):
        return lax.broadcasted_iota(jnp.int32, shape, axis).astype(F32)

    def column(value):
        return jnp.broadcast_to(value, (8, value.shape[1])).T[:, :1]

    row = row.astype(F32)
    square = (total, total)
    same = (column(row) == row) & (iota(square, 0) < iota(square, 1))
    within = jnp.sum(jnp.where(same, 1.0, 0.0), axis=0, keepdims=True)
    ids = iota((wide, total), 0)
    hit = (ids == row) & (ids < wanted_sources)
    count = jnp.sum(jnp.where(hit, 1.0, 0.0), axis=1, keepdims=True)
    need = jnp.floor((count + (QUAD - 1)) / QUAD)
    spread = jnp.broadcast_to(need, (wide, wide)).T
    before = iota((wide, wide), 1) < iota((wide, wide), 0)
    offset = jnp.sum(jnp.where(before, spread, 0.0), axis=1, keepdims=True)
    end = jnp.sum(spread[:1, :], axis=1, keepdims=True)
    base = jnp.sum(jnp.where(hit, QUAD * offset, 0.0), axis=0, keepdims=True)
    pos = jnp.where(row < wanted_sources, base + within, -1.0)
    here = column(pos) == iota((total, slots), 1)
    code = jnp.sum(jnp.where(here, iota((total, slots), 0) + 1.0, 0.0), axis=0, keepdims=True)
    q = iota((wide, quads), 1)
    inside = (offset <= q) & (q < offset + need)
    info = 2.0 * iota((wide, quads), 0) + jnp.where(offset == q, 1.0, 0.0)
    quad = jnp.sum(jnp.where(inside, info, 0.0), axis=0, keepdims=True)
    quad = jnp.where(q[:1, :] < end, quad, 2.0 * wanted_sources + 1.0)
    used = jnp.broadcast_to(jnp.floor((end + (STEP - 1)) / STEP), (1, 128))
    return code.astype(jnp.int32), quad.astype(jnp.int32), used.astype(jnp.int32)


def local_kernel(
    src,
    code,
    quad,
    used,
    feats,
    halo,
    stale,
    tiles,
    deg,
    w_self,
    w_neigh,
    cot,
    out,
    row_grad,
    halo_grad,
    part,
    tbuf,
    srcs,
    agg,
    back,
    grad,
    gt,
    sems,
):
    blocks = deg.shape[0]
    per = src.shape[1] // blocks
    tile, width = feats.shape[0] // blocks, feats.shape[1]
    n_halo, n_stale = halo.shape[0], stale.shape[0]

    def chunk(b):
        return pltpu.make_async_copy(
            tiles.at[pl.ds(b * per, per)], tbuf.at[pl.ds(b * per, per)], sems.at[b]
        )

    @pl.loop(0, blocks)
    def _(b):
        chunk(b).start()

    for b in range(blocks):
        srcs[b] = feats[b * tile : (b + 1) * tile, :]
    srcs[blocks : blocks + n_halo] = halo[...]
    srcs[blocks + n_halo :] = stale[...]
    grad[...] = jnp.zeros_like(grad)
    back[blocks] = jnp.zeros((width, tile), BF16)

    def forward(b):
        chunk(b).wait()
        lhs = jnp.concatenate([tbuf[b * per + t] for t in range(per)], axis=1)
        rhs = jnp.concatenate([srcs[src[0, b * per + t]] for t in range(per)], axis=0)
        total = jnp.dot(lhs, rhs, preferred_element_type=F32)
        d = jnp.broadcast_to(deg[pl.ds(b, 1), :].astype(F32), (tile, tile)).T
        agg[pl.ds(pl.multiple_of(b * tile, tile), tile), :] = (total / d).astype(BF16)

    pl.loop(0, blocks, unroll=2)(forward)

    gt[...] = jnp.zeros_like(gt)
    group = 8
    rows = group * tile
    w_cat = jnp.concatenate([w_self[...], w_neigh[...]], axis=0)

    def middle(c):
        at = pl.ds(pl.multiple_of(c * rows, rows), rows)
        fa = jnp.concatenate([feats[at, :], agg[at, :]], axis=1)
        pre = jnp.dot(fa, w_cat, preferred_element_type=F32)
        scale = lax.rsqrt(jnp.mean(pre * pre, axis=-1, keepdims=True) + 1e-05)
        out[at, :] = (pre * scale).astype(BF16)
        g = cot[at, :].astype(F32)
        m = jnp.mean(g * pre, axis=-1, keepdims=True)
        dpre = (scale * g - pre * (scale**3 * m)).astype(BF16)
        gt[...] += lax.dot_general(dpre, fa, (((0,), (0,)), ((), ())), preferred_element_type=F32)
        row_grad[at, :] = lax.dot_general(
            dpre, w_self[...], (((1,), (1,)), ((), ())), preferred_element_type=F32
        )
        bt = lax.dot_general(
            w_neigh[...], dpre, (((1,), (1,)), ((), ())), preferred_element_type=F32
        )
        for i in range(group):
            d = deg[pl.ds(c * group + i, 1), :].astype(F32)
            back[c * group + i] = (bt[:, i * tile : (i + 1) * tile] / d).astype(BF16)

    pl.loop(0, blocks // group)(middle)

    part[:width, :] = gt[:, :width].T
    part[width:, :] = gt[:, width:].T

    def backward(step, acc):
        terms = []
        for u in range(STEP):
            lhs, rhs = [], []
            for i in range(QUAD):
                k = code[0, (step * STEP + u) * QUAD + i]
                t = jnp.maximum(k - 1, 0)
                b = jnp.where(k == 0, blocks, t // per)
                lhs.append(back[b])
                rhs.append(tbuf[t])
            terms.append(
                jnp.dot(
                    jnp.concatenate(lhs, axis=1),
                    jnp.concatenate(rhs, axis=0),
                    preferred_element_type=F32,
                )
            )
        for u in range(STEP):
            info = quad[0, step * STEP + u]
            acc = terms[u] + jnp.where(info % 2 == 1, 0.0, acc)
            grad[info // 2] = acc
        return acc

    lax.fori_loop(0, used[0, 0], backward, jnp.zeros((width, tile), F32))

    def finish(b):
        at = pl.ds(pl.multiple_of(b * tile, tile), tile)
        row_grad[at, :] += grad[b].T

    pl.loop(0, blocks, unroll=4)(finish)
    for h in range(n_halo):
        halo_grad[h] = grad[blocks + h].T.astype(BF16)


def local(tile_src, plans, features, halo, stale, tiles, degree, w_self, w_neigh, cotangent):
    tile = tiles.shape[1]
    nodes, width = features.shape
    blocks = nodes // tile
    n_halo = halo.shape[0]
    smem = pl.BlockSpec(memory_space=pltpu.SMEM)
    vmem = pl.BlockSpec(memory_space=pltpu.VMEM)
    return pl.pallas_call(
        local_kernel,
        out_shape=(
            jax.ShapeDtypeStruct((nodes, width), BF16),
            jax.ShapeDtypeStruct((nodes, width), F32),
            jax.ShapeDtypeStruct((n_halo, tile, width), BF16),
            jax.ShapeDtypeStruct((2 * width, width), F32),
        ),
        in_specs=[smem] * 4
        + [vmem] * 3
        + [pl.BlockSpec(memory_space=pl.ANY)]
        + [vmem] * 4,
        out_specs=[vmem] * 4,
        scratch_shapes=[
            pltpu.VMEM(tiles.shape, BF16),
            pltpu.VMEM((blocks + n_halo + stale.shape[0], tile, width), BF16),
            pltpu.VMEM((nodes, width), BF16),
            pltpu.VMEM((blocks + 1, width, tile), BF16),
            pltpu.VMEM((blocks + n_halo + 1, width, tile), F32),
            pltpu.VMEM((width, 2 * width), F32),
            pltpu.SemaphoreType.DMA((blocks,)),
        ],
        compiler_params=pltpu.CompilerParams(vmem_limit_bytes=60 << 20),
    )(
        tile_src,
        *plans,
        features,
        halo,
        stale,
        tiles,
        degree.reshape(blocks, tile),
        w_self,
        w_neigh,
        cotangent,
    )


def greet(me_g, me_m, groups, members):
    barrier = pltpu.get_barrier_semaphore()
    for o in range(1, members):
        pl.semaphore_signal(
            barrier, inc=1, device_id=(me_g, lax.rem(me_m + o, members)), device_id_type=MESH
        )
    for o in range(1, groups):
        pl.semaphore_signal(
            barrier, inc=1, device_id=(lax.rem(me_g + o, groups), me_m), device_id_type=MESH
        )
    return lambda: pl.semaphore_wait(barrier, members + groups - 2)


def push(src, dst, send, recv, o, device):
    copy = pltpu.make_async_remote_copy(
        src_ref=src,
        dst_ref=dst,
        send_sem=send.at[o],
        recv_sem=recv.at[o],
        device_id=device,
        device_id_type=MESH,
    )
    copy.start()
    return copy


def pick_rows(row, table, depth):
    count = row.shape[1]
    column = jnp.broadcast_to(row, (8, count)).T[:, :1]
    total = jnp.zeros((count, table.shape[1]), F32)
    for c in range(0, table.shape[0], depth):
        ids = lax.broadcasted_iota(jnp.int32, (count, depth), 1) + c
        hot = jnp.where(ids == column, 1.0, 0.0).astype(BF16)
        total = total + jnp.dot(hot, table[c : c + depth, :], preferred_element_type=F32)
    return total


def gather_kernel(
    groups,
    members,
    feats_in,
    hist_in,
    rows,
    picks,
    stale_rows,
    tile_src,
    halo,
    stale,
    wanted,
    code,
    quad,
    used,
    asked,
    feats,
    hist,
    bound,
    outgoing,
    leaving,
    l_sems,
    p_send,
    p_recv,
    h_send,
    h_recv,
    s_send,
    s_recv,
):
    me_g, me_m = lax.axis_index("group"), lax.axis_index("member")
    taken = picks.shape[1]
    tile, width = halo.shape[1], halo.shape[2]
    offered = rows.shape[1] // tile
    each = stale_rows.shape[1] // tile
    depth = 512
    load_feats = pltpu.make_async_copy(feats_in, feats, l_sems.at[0])
    load_hist = pltpu.make_async_copy(hist_in, hist, l_sems.at[1])
    load_feats.start()
    load_hist.start()
    for p in range(members):
        for k in range(taken):
            asked[p, k] = jnp.broadcast_to(picks[p : p + 1, k : k + 1], asked.shape[2:])
    entered = greet(me_g, me_m, groups, members)
    wanted[me_m] = asked[me_m]
    load_feats.wait()
    bound[...] = pick_rows(rows[...], feats, depth).reshape(offered, tile, width)
    entered()
    load_hist.wait()
    copies, calls = [], []
    for o in range(1, members):
        peer = lax.rem(me_m + o, members)
        calls.append(
            push(asked.at[peer], wanted.at[me_m], p_send, p_recv, o, (me_g, peer))
        )

    def send_stale(o):
        to = lax.rem(me_g + o, groups)
        found = pick_rows(stale_rows[pl.ds(to, 1), :], hist, depth)
        found = found.astype(BF16).reshape(each, tile, width)
        at = pl.ds(me_g * each, each)
        if o == 0:
            stale[at] = found
        else:
            leaving[o] = found
            copies.append(push(leaving.at[o], stale.at[at], s_send, s_recv, o, (to, me_m)))

    def choose(p, k):
        w = jnp.broadcast_to(wanted[p, k][:1, :], (tile, width))
        value = bound[0]
        for j in range(1, offered):
            value = jnp.where(w == j, bound[j], value)
        return value.astype(BF16)

    for o in range(groups - 1, 1, -1):
        send_stale(o)
    for o in range(1, members):
        calls[o - 1].wait_recv()
        peer = lax.rem(me_m + members - o, members)
        for k in range(taken):
            outgoing[o, k] = choose(peer, k)
        at = pl.ds(me_m * taken, taken)
        copies.append(push(outgoing.at[o], halo.at[at], h_send, h_recv, o, (me_g, peer)))
    for k in range(taken):
        halo[me_m * taken + k] = choose(me_m, k)
    if groups > 1:
        send_stale(1)
    send_stale(0)
    blocks = feats.shape[0] // tile
    code[...], quad[...], used[...] = plan(
        tile_src[...], blocks + members * taken, code.shape[1], quad.shape[1]
    )
    for copy in calls:
        copy.wait_send()
    for copy in copies:
        copy.wait()


def gather(features, history, boundary_rows, picks, stale_rows, tile_src, tile, groups, members):
    taken = picks.shape[1]
    width = features.shape[1]
    offered = boundary_rows.shape[1] // tile
    each = stale_rows.shape[1] // tile
    wanted_sources = features.shape[0] // tile + members * taken
    slots, quads = plan_sizes(tile_src.shape[1], wanted_sources)
    vmem = pl.BlockSpec(memory_space=pltpu.VMEM)
    dma = pltpu.SemaphoreType.DMA
    return pl.pallas_call(
        functools.partial(gather_kernel, groups, members),
        out_shape=(
            jax.ShapeDtypeStruct((members * taken, tile, width), BF16),
            jax.ShapeDtypeStruct((groups * each, tile, width), BF16),
            jax.ShapeDtypeStruct((members, taken, 8, 128), jnp.int32),
            jax.ShapeDtypeStruct((1, slots), jnp.int32),
            jax.ShapeDtypeStruct((1, quads), jnp.int32),
            jax.ShapeDtypeStruct((1, 128), jnp.int32),
        ),
        in_specs=[pl.BlockSpec(memory_space=pl.ANY)] * 2 + [vmem] * 4,
        out_specs=[vmem] * 6,
        scratch_shapes=[
            pltpu.VMEM((members, taken, 8, 128), jnp.int32),
            pltpu.VMEM(features.shape, BF16),
            pltpu.VMEM(history.shape, BF16),
            pltpu.VMEM((offered, tile, width), F32),
            pltpu.VMEM((members, taken, tile, width), BF16),
            pltpu.VMEM((groups, each, tile, width), BF16),
            dma((2,)),
            dma((members,)),
            dma((members,)),
            dma((members,)),
            dma((members,)),
            dma((groups,)),
            dma((groups,)),
        ],
        compiler_params=pltpu.CompilerParams(
            collective_id=0, has_side_effects=True, vmem_limit_bytes=60 << 20
        ),
    )(features, history, boundary_rows, picks, stale_rows, tile_src)


def combine_kernel(
    groups,
    members,
    row_grad_in,
    halo_grad,
    part,
    wanted,
    rows,
    grad_features,
    grads,
    row_grad,
    l_sem,
    returned,
    landed,
    partial,
    across,
    share,
    whole,
    h_send,
    h_recv,
    a_send,
    a_recv,
    b_send,
    b_recv,
    c_send,
    c_recv,
):
    me_g, me_m = lax.axis_index("group"), lax.axis_index("member")
    taken = wanted.shape[1]
    nodes, width = row_grad.shape
    tile = halo_grad.shape[1]
    offered = rows.shape[1] // tile
    piece = part.shape[0] // members
    load = pltpu.make_async_copy(row_grad_in, row_grad, l_sem)
    load.start()
    greet(me_g, me_m, groups, members)()
    copies, first, second, third = [], [], [], []
    for o in range(1, members):
        peer = lax.rem(me_m + o, members)
        at = pl.ds(pl.multiple_of(peer * piece, piece), piece)
        first.append(
            push(part.at[at], landed.at[me_m], a_send, a_recv, o, (me_g, peer))
        )
    for o in range(1, members):
        peer = lax.rem(me_m + o, members)
        copies.append(
            push(
                halo_grad.at[pl.ds(peer * taken, taken)],
                returned.at[me_m],
                h_send,
                h_recv,
                o,
                (me_g, peer),
            )
        )
    landed[me_m] = part[pl.ds(pl.multiple_of(me_m * piece, piece), piece), :]
    returned[me_m] = halo_grad[pl.ds(me_m * taken, taken)]
    for copy in first:
        copy.wait_recv()
    total = landed[0]
    for p in range(1, members):
        total = total + landed[p]
    partial[...] = total
    across[me_g] = total
    for o in range(1, groups):
        to = lax.rem(me_g + o, groups)
        second.append(push(partial, across.at[me_g], b_send, b_recv, o, (to, me_m)))
    for copy in second:
        copy.wait_recv()
    total = across[0]
    for g in range(1, groups):
        total = total + across[g]
    mine = pl.ds(pl.multiple_of(me_m * piece, piece), piece)
    share[...] = total
    whole[mine, :] = total
    for o in range(1, members):
        peer = lax.rem(me_m + o, members)
        third.append(push(share, whole.at[mine], c_send, c_recv, o, (me_g, peer)))

    for copy in copies:
        copy.wait_recv()
    halves = []
    for j in range(offered):
        total = jnp.zeros((tile, width), F32)
        for p in range(members):
            for k in range(taken):
                w = jnp.broadcast_to(wanted[p, k][:1, :], (tile, width))
                total = total + jnp.where(w == j, returned[p, k].astype(F32), 0.0)
        high = total.astype(BF16)
        low = (total - high.astype(F32)).astype(BF16)
        halves.append(jnp.concatenate([high, low], axis=1))
    extra = jnp.concatenate(halves, axis=0)
    load.wait()
    depth = 512

    def add(c):
        at = pl.ds(pl.multiple_of(c * depth, depth), depth)
        ids = lax.broadcasted_iota(jnp.int32, (depth, rows.shape[1]), 0) + c * depth
        hot = jnp.where(ids == rows[...], 1.0, 0.0).astype(BF16)
        more = jnp.dot(hot, extra, preferred_element_type=F32)
        grad_features[at, :] = (row_grad[at, :] + (more[:, :width] + more[:, width:])).astype(BF16)

    pl.loop(0, nodes // depth)(add)
    for copy in third:
        copy.wait_recv()
    grads[...] = whole[...]
    for copy in first + second + third + copies:
        copy.wait_send()


def combine(row_grad, halo_grad, part, wanted, boundary_rows, groups, members):
    nodes, width = row_grad.shape
    tile = halo_grad.shape[1]
    taken = wanted.shape[1]
    piece = part.shape[0] // members
    vmem = pl.BlockSpec(memory_space=pltpu.VMEM)
    dma = pltpu.SemaphoreType.DMA
    return pl.pallas_call(
        functools.partial(combine_kernel, groups, members),
        out_shape=(
            jax.ShapeDtypeStruct((nodes, width), BF16),
            jax.ShapeDtypeStruct(part.shape, F32),
        ),
        in_specs=[pl.BlockSpec(memory_space=pl.ANY)] + [vmem] * 4,
        out_specs=[vmem] * 2,
        scratch_shapes=[
            pltpu.VMEM((nodes, width), F32),
            dma(()),
            pltpu.VMEM((members, taken, tile, width), BF16),
            pltpu.VMEM((members, piece, part.shape[1]), F32),
            pltpu.VMEM((piece, part.shape[1]), F32),
            pltpu.VMEM((groups, piece, part.shape[1]), F32),
            pltpu.VMEM((piece, part.shape[1]), F32),
            pltpu.VMEM(part.shape, F32),
            dma((members,)),
            dma((members,)),
            dma((members,)),
            dma((members,)),
            dma((groups,)),
            dma((groups,)),
            dma((members,)),
            dma((members,)),
        ],
        compiler_params=pltpu.CompilerParams(
            collective_id=1, has_side_effects=True, vmem_limit_bytes=60 << 20
        ),
    )(row_grad, halo_grad, part, wanted, boundary_rows)


def on_device(
    features,
    history,
    tiles,
    tile_src,
    degree,
    boundary_rows,
    picks,
    stale_rows,
    w_self,
    w_neigh,
    cotangent,
):
    members = lax.axis_size("member")
    groups = lax.axis_size("group")
    tile = tiles.shape[1]
    tile_src = tile_src.reshape(1, -1)
    halo, stale, wanted, *plans = gather(
        features, history, boundary_rows, picks, stale_rows, tile_src, tile, groups, members
    )
    layer_out, row_grad, halo_grad, part = local(
        tile_src, plans, features, halo, stale, tiles, degree, w_self, w_neigh, cotangent
    )
    factor = 1.0 / math.sqrt(features.shape[0] * members * groups)
    grad_features, grads = combine(
        row_grad, halo_grad, part, wanted, boundary_rows, groups, members
    )
    width = features.shape[1]
    return (layer_out, grad_features, grads[:width] * factor, grads[width:] * factor)


def solution(mesh):
    placed = (
        P(("group", "member"), None),
        P(("group", "member"), None),
        P(("group", "member"), None, None),
        P(("group", "member"), None),
        P(("group", "member")),
        P(("group", "member"), None),
        P(("group", "member"), None),
        P(("group", "member"), None),
        P(),
        P(),
        P(("group", "member"), None),
    )
    return jax.shard_map(
        on_device,
        mesh=mesh,
        in_specs=placed,
        out_specs=(P(("group", "member"), None), P(("group", "member"), None), P(), P()),
        check_vma=False,
    )
```
